256 devices in a mesh: ctx: 32 (over y, z), head: 8 (over x, core).
Axes of the slice: x: 4, y: 4, z: 8, core: 2. Of those that a mesh axis runs over, the one named last changes fastest.
Arguments:
- enc_rows: bfloat16 [16384, 1024], P(('ctx', 'head')), may hold values from -6 to 6
- row_counts: int32 [32, 8], P('ctx'), may hold values from 0 to 64, as said below
- row_places: int32 [32, 512], P('ctx'), may hold values from 0 to 16383, as said below
- stream: bfloat16 [16384, 3072], P('ctx'), may hold values from -134 to 134
- norm_gain: float32 [3072], replicated, may hold values from 0.25 to 1.75
- proj_in: bfloat16 [1024, 6144], P('ctx', 'head'), may hold values from -0.1875 to 0.1875
- proj_out: bfloat16 [6144, 3072], P('head', 'ctx'), may hold values from -0.078125 to 0.078125
- qkv_weight: bfloat16 [3072, 3, 4096], P(None, None, 'head'), may hold values from -0.109375 to 0.109375
- head_gain: float32 [4096], P('head'), may hold values from 0.25 to 1.75
- mix_weight: bfloat16 [4096, 3072], P('head', 'ctx'), may hold values from -0.09375 to 0.09375
Outputs:
- layer_out: bfloat16 [16384, 3072], P('ctx', 'head')
The draws below stay inside these ranges and needn't reach their ends.
Inputs may be any that keep to these rules, and one draw needn't show every extreme that they name: `row_counts`: the 8 devices of one ctx index hold 128 live rows together, and some device holds 64. `row_places`: the place of a live slot of a device with ctx index c lies from c * 512 to c * 512 + 511, and live places are distinct; a slot that is not live holds a place in the same range, which is ignored.
All inputs are finite; a program needn't handle non-finite values.
Results may differ from the reference program's by a relative error of at most 0.015.
Values may be sent and summed in bfloat16 or wider, within the bound.
A program may use at most 128 MiB of HBM per device.

```python
import math
import jax
import jax.numpy as jnp
from jax import lax

ENC = 1024
PROJ = 6144
D = 3072
HEAD_DIM = 128
HEADS_DEV = 4
SHARD = 512
HEADS = 32
CAP = 64
BLOCK = 512
TOKENS = 16384
SLOTS = 16384
N_CTX = 32
N_HEAD = 8


def layout(seed_key):
    base_key = jax.random.fold_in(seed_key, 7)
    key_cuts, key_pick, key_perm, key_pos, key_fill = jax.random.split(base_key, 5)
    quad_count = N_CTX * N_HEAD // 4
    cut_points = jax.random.randint(key_cuts, (quad_count, 3), 0, CAP + 1)
    chosen = jax.random.randint(key_pick, (), 0, quad_count)
    cut_points = jnp.where(jnp.arange(quad_count)[:, None] == chosen, CAP, cut_points)
    cut_points = jnp.sort(cut_points, axis=1).astype(jnp.int32)
    edge_points = jnp.concatenate([jnp.zeros((quad_count, 1), jnp.int32), cut_points, jnp.full((quad_count, 1), CAP, jnp.int32)], axis=1)
    row_parts = edge_points[:, 1:] - edge_points[:, :-1]
    ranking = jax.random.randint(key_perm, (quad_count, 4), 0, 1 << 20) * 4 + jnp.arange(4)
    row_parts = jnp.take_along_axis(row_parts, jnp.argsort(ranking, axis=1), axis=1)
    counts = row_parts.reshape(N_CTX, N_HEAD).astype(jnp.int32)
    starts = jnp.cumsum(counts, axis=1) - counts
    slot_index = jnp.arange(CAP, dtype=jnp.int32)
    row_rank = starts[:, :, None] + slot_index[None, None, :]
    is_live = (slot_index[None, None, :] < counts[:, :, None]).reshape(N_CTX, N_HEAD * CAP)
    ranking_pos = jax.random.randint(key_pos, (N_CTX, SHARD), 0, 1 << 20) * SHARD + jnp.arange(SHARD)
    offsets = jnp.argsort(ranking_pos, axis=1).astype(jnp.int32)
    safe_rank = jnp.minimum(row_rank, SHARD - 1).reshape(N_CTX, N_HEAD * CAP).astype(jnp.int32)
    picked = jnp.take_along_axis(offsets, safe_rank, axis=1)
    filler = jax.random.randint(key_fill, (N_CTX, N_HEAD * CAP), 0, SHARD)
    local_place = jnp.where(is_live, picked, filler)
    places = local_place + jnp.arange(N_CTX)[:, None] * SHARD
    return (counts, places.astype(jnp.int32))


def draw_row_counts(key, part):
    counts, places = layout(key)
    return counts


def draw_row_places(key, part):
    counts, places = layout(key)
    return places


def draw_stream(key, part):
    base_key = jax.random.fold_in(key, 11)
    key_main, key_cols, key_rows = jax.random.split(base_key, 3)
    column_scale = jnp.exp(jax.random.uniform(key_cols, (D,), jnp.float32, 0.0, math.log(10.0)))
    row_scale = jnp.exp(jax.random.uniform(key_rows, (TOKENS, 1), jnp.float32, 0.0, math.log(10.0)))
    entries = jnp.clip(jax.random.normal(key_main, (TOKENS, D), jnp.float32), -4.0, 4.0)
    return (entries * column_scale * row_scale / 3.0).astype(jnp.bfloat16)


def levels(key, extent, pieces, least, high):
    def one(axis_at, parts):
        draws = jax.random.uniform(jax.random.fold_in(jax.random.fold_in(key, 6), axis_at), (parts,), jnp.float32, least / len(pieces), high / len(pieces))
        return jnp.repeat(jnp.exp(draws), extent[axis_at] // parts).reshape((-1,) + (1,) * (len(extent) - axis_at - 1))

    factor_of = one(*pieces[0])
    for cut in pieces[1:]:
        factor_of = factor_of * one(*cut)
    return factor_of


def noise(own_key, shape, width, bound, pieces=(), held_as=jnp.bfloat16):
    gain = levels(own_key, shape, pieces, -0.22, 0.18) if pieces else 1.0
    drawn = jax.random.normal(own_key, shape, jnp.float32) * width * gain
    return jnp.minimum(jnp.maximum(drawn, -bound), bound).astype(held_as)


def setup_inputs(seed: int = 0) -> dict:
    key_list = jax.random.split(jax.random.key(seed), 11)
    return {
        "enc_rows": noise(key_list[0], (SLOTS, ENC), 1.0, 6.0, ((0, 256),)),
        "row_counts": draw_row_counts(jax.random.fold_in(key_list[10], 71), 0),
        "row_places": draw_row_places(jax.random.fold_in(key_list[10], 71), 0),
        "stream": draw_stream(jax.random.fold_in(key_list[10], 71), 0),
        "norm_gain": jnp.clip(1.0 + 0.15 * jax.random.normal(key_list[4], (D,), jnp.float32), 0.25, 1.75),
        "proj_in": noise(key_list[5], (ENC, PROJ), ENC ** -0.5, 0.1875, ((0, 32), (1, 8))),
        "proj_out": noise(key_list[6], (PROJ, D), PROJ ** -0.5, 0.078125, ((0, 8), (1, 32))),
        "qkv_weight": noise(key_list[7], (D, 3, HEADS * HEAD_DIM), D ** -0.5, 0.109375, ((2, 8),)),
        "head_gain": jnp.clip(1.0 + 0.15 * jax.random.normal(key_list[8], (HEADS * HEAD_DIM,), jnp.float32), 0.25, 1.75),
        "mix_weight": noise(key_list[9], (HEADS * HEAD_DIM, D), (HEADS * HEAD_DIM) ** -0.5, 0.09375, ((0, 8), (1, 32))),
    }


def reference(enc_rows, row_counts, row_places, stream, norm_gain, proj_in, proj_out, qkv_weight, head_gain, mix_weight):
    slot_index = jnp.arange(SLOTS, dtype=jnp.int32)
    owner_dev = slot_index // CAP
    within = slot_index % CAP
    flat_counts = row_counts.reshape(N_CTX * N_HEAD)
    is_live = within < flat_counts[owner_dev]
    targets = jnp.where(is_live, row_places.reshape(SLOTS), TOKENS).astype(jnp.int32)
    hidden = jax.nn.gelu(jnp.dot(enc_rows, proj_in, preferred_element_type=jnp.float32), approximate=False).astype(jnp.bfloat16)
    image_rows = jnp.dot(hidden, proj_out, preferred_element_type=jnp.float32).astype(jnp.bfloat16)
    packed = stream.at[targets].set(image_rows, mode='drop')
    flat_qkv = qkv_weight.reshape(D, 3 * HEADS * HEAD_DIM)
    wide_mix = mix_weight.astype(jnp.float32).reshape(N_HEAD, HEADS_DEV * HEAD_DIM, D)
    causal = jnp.tril(jnp.ones((BLOCK, BLOCK), dtype=bool))
    blocks = packed.reshape(TOKENS // BLOCK, BLOCK, D)
    highest = lax.Precision.HIGHEST

    def advance(carried, block_rows):
        widened = block_rows.astype(jnp.float32)
        normed = (widened * lax.rsqrt(lax.optimization_barrier(jnp.mean(widened * widened, axis=-1, keepdims=True)) + 1e-05) * norm_gain).astype(jnp.bfloat16)
        projected = jax.nn.silu(jnp.dot(normed, flat_qkv, preferred_element_type=jnp.float32)).astype(jnp.bfloat16)
        projected = lax.optimization_barrier(projected)
        projected = projected.reshape(BLOCK, 3, HEADS, HEAD_DIM).astype(jnp.float32)
        queries = projected[:, 0]
        key_rows = projected[:, 1]
        values = projected[:, 2]
        scores = jnp.einsum('qhd,khd->hqk', queries, key_rows, precision=highest)
        scores = jnp.where(causal[None], scores, 0.0).astype(jnp.bfloat16)
        scores = lax.optimization_barrier(scores).astype(jnp.float32)
        attended = jnp.einsum('hqk,khd->qhd', scores, values, precision=highest)
        attended = attended + jnp.einsum('qhd,hde->qhe', queries, carried, precision=highest)
        carried = carried + jnp.einsum('khd,khe->hde', key_rows, values, precision=highest)
        inverse_rms = lax.rsqrt(lax.optimization_barrier(jnp.mean(attended * attended, axis=-1, keepdims=True)) + 1e-06)
        heads_out = (attended * inverse_rms * head_gain.reshape(HEADS, HEAD_DIM)).astype(jnp.bfloat16)
        heads_out = lax.optimization_barrier(heads_out)
        grouped = heads_out.reshape(BLOCK, N_HEAD, HEADS_DEV * HEAD_DIM).astype(jnp.float32)
        partials = jnp.einsum('tgc,gcd->tgd', grouped, wide_mix, precision=highest).astype(jnp.bfloat16)
        partials = lax.optimization_barrier(partials).astype(jnp.float32)
        return (carried, lax.optimization_barrier(jnp.sum(partials, axis=1)).astype(jnp.bfloat16))
    initial = jnp.zeros((HEADS, HEAD_DIM, HEAD_DIM), jnp.float32)
    _, outputs = lax.scan(advance, initial, blocks)
    return outputs.reshape(TOKENS, D)
```

```python
import heapq

import jax
import jax.numpy as jnp
from jax import lax
from jax.experimental import pallas as pl
from jax.experimental.pallas import tpu as pltpu
from jax.sharding import PartitionSpec as P

MESH = pl.DeviceIdType.MESH
BF16 = jnp.bfloat16
F32 = jnp.float32
VMEM_BYTES = 64 * 1024 * 1024 - 65536

PIECES = (
    (0, "a", 0, 32, 32, 1536),
    (1, "a", 0, 48, 96, 1536),
    (1, "b", 48, 48, 96, 1536),
    (2, "a", 0, 64, 96, 1024),
    (2, "b", 64, 32, 96, 1024),
)
RELEASE = (0, 0, 0, 90, 90)


def forwards(tree, dy, dz):
    out = []
    if tree == "a":
        if dy == 0:
            if dz == 0:
                out += [("z+", (0, -1)), ("z-", (0, 1))]
            elif -4 < dz < 0:
                out.append(("z+", (0, dz - 1)))
            elif 0 < dz < 3:
                out.append(("z-", (0, dz + 1)))
            out += [("y+", (-1, dz)), ("y-", (1, dz))]
        elif dy == -1 and dz % 2 == 0:
            out.append(("y+", (-2, dz)))
        elif dy == 1 and dz % 2 != 0:
            out.append(("y-", (-2, dz)))
    else:
        if dz == 0:
            if dy == 0:
                out += [("y+", (-1, 0)), ("y-", (1, 0))]
            elif dy == -1:
                out.append(("y+", (-2, 0)))
            out += [("z+", (dy, -1)), ("z-", (dy, 1))]
        elif -4 < dz < 0:
            out.append(("z+", (dy, dz - 1)))
        elif 0 < dz < 3:
            out.append(("z-", (dy, dz + 1)))
    return out


def plan():
    rate, hop = 46.5e3, 1.8
    free = dict.fromkeys(("z+", "z-", "y+", "y-"), 0.0)
    now, count, order, heap = 0.0, 0, [], []
    released = set()
    tasks = [(("norm", i), 0.4) for i in range(8)] + [(("stream", i), 1.75) for i in range(6)]
    need = {dy: 16 for dy in (0, -1, 1, -2)}
    need[0] -= 2
    left_a, hid_done, ready, parts = 31, False, [], 0
    for at, name in ((4.8, "enc1"), (7.5, "enc2"), (10.0, "enc3")):
        heapq.heappush(heap, (at, ("x", name)))

    def issue(p, dy, dz):
        _, tree, _, rows, _, width = PIECES[p]
        for link, target in forwards(tree, dy, dz):
            free[link] = max(free[link], now) + rows * width / rate
            heapq.heappush(heap, (free[link] + hop, ("rx", p) + target))

    while True:
        for p in range(len(PIECES)):
            if p not in released and count >= RELEASE[p]:
                released.add(p)
                order.append(("own", p))
                issue(p, 0, 0)
        if heap and heap[0][0] <= now:
            event = heapq.heappop(heap)[1]
            order.append(event)
            if event[0] == "rx":
                _, p, dy, dz = event
                count += 1
                issue(p, dy, dz)
                if p == 0:
                    left_a -= 1
                elif p < 3:
                    need[dy] -= 1
                    if need[dy] == 0:
                        ready.append(dy)
            elif event[1] == "rsum":
                now += 0.5
                heapq.heappush(heap, (now + 4.5, ("x", "ag1")))
                heapq.heappush(heap, (now + 6.8, ("x", "ag2")))
                heapq.heappush(heap, (now + 8.0, ("x", "ag3")))
            elif event[1] == "ag3":
                tasks += [(("image", i), 0.9) for i in range(3)]
            continue
        if left_a == 0 and not hid_done and ("x", "enc3") in order:
            order.append(("hid",))
            hid_done = True
            now += 1.2
            continue
        if hid_done and ready:
            order.append(("part", ready.pop(0)))
            now += 0.5
            parts += 1
            if parts == 4:
                heapq.heappush(heap, (now + 3.0, ("x", "rsum")))
            continue
        if tasks:
            task, time = tasks.pop(0)
            order.append(task)
            now += time
            continue
        if not heap:
            return order
        now = max(now, heap[0][0])


ORDER = plan()


def dot(a, b, dims):
    return lax.dot_general(a, b, (dims, ((), ())), preferred_element_type=F32)


def silu(v):
    return v * jax.nn.sigmoid(v)


def live_slots(counts_ref):
    slot = lax.broadcasted_iota(jnp.int32, (8, 512), 1)
    rank = jnp.full((8, 512), -1, jnp.int32)
    before = jnp.int32(0)
    for h in range(8):
        count = counts_ref[0, h]
        within = slot - 64 * h
        mine = (within >= 0) & (within < 64) & (within < count)
        rank = jnp.where(mine, within + before, rank)
        before = before + count
    return rank


def place_of_me():
    c, h = lax.axis_index("ctx"), lax.axis_index("head")
    y, z, x, core = c // 8, c % 8, h // 2, h % 2
    return c, h, y, z, x, core, 1 - 2 * core


def first_kernel(
    counts, enc, stream, gain, a_in, b_in, c_in, w_in,
    out_s, out_i, mix,
    buf_a, buf_b, wq, xs, encb, hid, pbuf, rbuf, nbuf,
    lsem, wsem, ssem, rsem, es, er, ps, pr, gs, gr,
):
    c, h, y, z, x, core, s = place_of_me()
    bufs = (buf_a, buf_b, mix)
    own = []
    for i, (src, buf, rows) in enumerate(((a_in, buf_a, 32), (b_in, buf_b, 96), (c_in, mix, 96))):
        own.append(
            pltpu.make_async_copy(src, buf.at[pl.ds(pl.multiple_of(c * rows, 32), rows)], lsem.at[i])
        )
    load_x = pltpu.make_async_copy(stream, xs, lsem.at[3])
    own.append(pltpu.make_async_copy(enc, encb.at[h], lsem.at[4]))
    load_w = [pltpu.make_async_copy(w_in.at[i], wq.at[i], wsem.at[i]) for i in range(3)]
    for copy in own:
        copy.start()
    load_x.start()
    for copy in load_w:
        copy.start()

    def ctx_at(dy, dz):
        return lax.rem(y + s * dy + 8, 4) * 8 + lax.rem(z + s * dz + 16, 8)

    links = {"z+": ctx_at(0, 1), "z-": ctx_at(0, -1), "y+": ctx_at(1, 0), "y-": ctx_at(-1, 0)}
    barrier = pltpu.get_barrier_semaphore()
    for link in links.values():
        pl.semaphore_signal(barrier, inc=1, device_id=(link, h), device_id_type=MESH)
    for k in range(1, 8):
        pl.semaphore_signal(
            barrier, inc=1, device_id=(c, lax.rem(h + k, 8)), device_id_type=MESH
        )
    pl.semaphore_wait(barrier, 11)
    for copy in own:
        copy.wait()

    def chunk(p, dy, dz):
        b, _, first, rows, shard, _ = PIECES[p]
        row = pl.multiple_of(ctx_at(dy, dz) * shard + first, 16)
        return bufs[b].at[pl.ds(row, rows)]

    def index(dy, dz):
        return (dy + 2) * 8 + dz + 4

    def spread(p, dy, dz):
        ref = chunk(p, dy, dz)
        for link, target in forwards(PIECES[p][1], dy, dz):
            pltpu.make_async_remote_copy(
                ref, ref, ssem.at[p], rsem.at[p, index(*target)],
                device_id=(links[link], h), device_id_type=MESH,
            ).start()

    def arrived(p, dy, dz):
        ref = chunk(p, dy, dz)
        pltpu.make_async_remote_copy(
            ref, ref, ssem.at[p], rsem.at[p, index(dy, dz)],
            device_id=(links["z+"], h), device_id_type=MESH,
        ).wait_recv()

    sib = 2 * x + 1 - core
    xp = 2 * lax.rem(x + s + 4, 4) + core
    xm = 2 * lax.rem(x - s + 4, 4) + core
    xd = 2 * lax.rem(x + 2, 4) + core

    def over_head(refs, sends, recvs):
        def push(owner, to, n, slot):
            pltpu.make_async_remote_copy(
                refs(owner), refs(owner), sends.at[n], recvs.at[slot],
                device_id=(c, to), device_id_type=MESH,
            ).start()

        def take(owner, slot):
            pltpu.make_async_remote_copy(
                refs(owner), refs(owner), sends.at[0], recvs.at[slot],
                device_id=(c, sib), device_id_type=MESH,
            ).wait_recv()

        def begin():
            push(h, xp, 0, 1)
            push(h, xm, 1, 2)
            push(h, sib, 2, 4)

        def one():
            take(xm, 1)
            push(xm, xp, 3, 3)
            push(xm, sib, 4, 5)
            take(xp, 2)
            push(xp, sib, 5, 6)

        def two():
            take(xd, 3)
            push(xd, sib, 6, 7)

        def three():
            for slot, owner in ((4, sib), (5, sib), (6, sib), (7, sib)):
                take(owner, slot)

        def drain():
            for n in range(7):
                pltpu.make_async_remote_copy(
                    refs(h), refs(h), sends.at[n], recvs.at[0],
                    device_id=(c, sib), device_id_type=MESH,
                ).wait_send()

        return begin, one, two, three, drain

    enc_steps = over_head(lambda o: encb.at[o], es, er)
    ag_steps = over_head(lambda o: nbuf.at[pl.ds(pl.multiple_of(o * 16, 16), 16)], gs, gr)
    enc_steps[0]()

    def norm(v):
        return v * lax.rsqrt(jnp.mean(v * v, axis=-1, keepdims=True) + 1e-05) * gain[...]

    def columns(dy):
        return pl.ds(pl.multiple_of(lax.rem(y + s * dy + 8, 4) * 768, 768), 768)

    for event in ORDER:
        kind = event[0]
        if kind == "own":
            spread(event[1], 0, 0)
        elif kind == "rx":
            arrived(*event[1:])
            spread(*event[1:])
        elif kind == "norm":
            if event[1] == 0:
                load_x.wait()
            rows = pl.ds(64 * event[1], 64)
            xs[rows, :] = norm(xs[rows, :].astype(F32)).astype(BF16)
        elif kind == "stream":
            i, half = divmod(event[1], 2)
            if half == 0:
                load_w[i].wait()
            w = wq[i, :, pl.ds(256 * half, 256)]
            value = silu(dot(xs[...], w, ((1,), (0,))))
            out_s[:, pl.ds(512 * i + 256 * half, 256)] = value.astype(BF16)
        elif kind == "image":
            i = event[1]
            value = silu(dot(nbuf[...], wq[i], ((1,), (0,))))
            out_i[:, pl.ds(512 * i, 512)] = value.astype(BF16)
        elif kind == "hid":
            rank = live_slots(counts)
            row = lax.broadcasted_iota(jnp.int32, (128, 512), 0)
            pick = jnp.where(row == rank[0:1, :], 1.0, 0.0).astype(BF16)
            rows = dot(pick, encb[...].reshape(512, 1024), ((1,), (0,))).astype(BF16)
            u = dot(rows, buf_a[...], ((1,), (0,)))
            hid[...] = (0.5 * u * (1.0 + lax.erf(u * 0.7071067811865476))).astype(BF16)
        elif kind == "part":
            f = event[1] + 2
            cols = columns(event[1])
            pbuf[:, cols] = dot(hid[...], buf_b[cols, :], ((1,), (1,))).astype(BF16)
            for k in range(1, 8):
                to = lax.rem(h + k, 8)
                pltpu.make_async_remote_copy(
                    pbuf.at[pl.ds(pl.multiple_of(to * 16, 16), 16), cols],
                    rbuf.at[h, :, cols], ps.at[f], pr.at[h, f],
                    device_id=(c, to), device_id_type=MESH,
                ).start()
        elif event[1] == "enc1":
            enc_steps[1]()
        elif event[1] == "enc2":
            enc_steps[2]()
        elif event[1] == "enc3":
            enc_steps[3]()
        elif event[1] == "rsum":
            mine = pl.ds(pl.multiple_of(h * 16, 16), 16)
            total = pbuf[mine, :].astype(F32)
            for k in range(1, 8):
                frm = lax.rem(h + k, 8)
                for f in range(4):
                    ref = rbuf.at[frm, :, pl.ds(768 * f, 768)]
                    pltpu.make_async_remote_copy(
                        ref, ref, ps.at[f], pr.at[frm, f], device_id=(c, frm), device_id_type=MESH
                    ).wait_recv()
                total = total + rbuf[frm].astype(F32)
            nbuf[mine, :] = norm(total.astype(BF16).astype(F32)).astype(BF16)
            ag_steps[0]()
        elif event[1] == "ag1":
            ag_steps[1]()
        elif event[1] == "ag2":
            ag_steps[2]()
        elif event[1] == "ag3":
            ag_steps[3]()

    for p, (b, _, _, rows, _, _) in enumerate(PIECES):
        ref = bufs[b].at[pl.ds(0, 31 * rows)]
        pltpu.make_async_remote_copy(
            ref, ref, ssem.at[p], rsem.at[p, 0], device_id=(links["z+"], h), device_id_type=MESH
        ).wait_send()
    for f in range(4):
        ref = pbuf.at[pl.ds(0, 112), pl.ds(0, 768)]
        pltpu.make_async_remote_copy(
            ref, ref, ps.at[f], pr.at[0, f], device_id=(c, sib), device_id_type=MESH
        ).wait_send()
    enc_steps[4]()
    ag_steps[4]()


def second_kernel(
    counts, places, q_s, q_i, hg, mix,
    out,
    qkv, st_s, st_r, y_s, y_r, pre_s, pre, att, ho, part, sibb, pair, chain, fin,
    sem_s, sem_r, ysem_s, ysem_r, psem_s, psem_r, bsem_s, bsem_r, csem_s, csem_r,
):
    c, h, y, z, x, core, s = place_of_me()
    sib = 2 * x + 1 - core
    xp = 2 * lax.rem(x + s + 4, 4) + core
    xm = 2 * lax.rem(x - s + 4, 4) + core
    barrier = pltpu.get_barrier_semaphore()
    for k in range(1, 8):
        pl.semaphore_signal(
            barrier, inc=1, device_id=(y * 8 + lax.rem(z + k, 8), h), device_id_type=MESH
        )
    for k in range(1, 4):
        pl.semaphore_signal(
            barrier, inc=1, device_id=(lax.rem(y + k, 4) * 8 + z, h), device_id_type=MESH
        )
    for to in (sib, xp, xm):
        pl.semaphore_signal(barrier, inc=1, device_id=(c, to), device_id_type=MESH)

    rank = live_slots(counts)[0:1, :]
    row = lax.broadcasted_iota(jnp.int32, (128, 512), 0)
    local = places[...] - c * 512
    where = jnp.sum(jnp.where(row == rank, local, 0).astype(F32), axis=1, keepdims=True)
    token = lax.broadcasted_iota(jnp.int32, (128, 512), 1)
    put = jnp.where(token == where.astype(jnp.int32), 1.0, 0.0).astype(BF16)
    hit = dot(put, jnp.ones((128, 128), BF16), ((0,), (0,)))[:, 0:1] > 0.5
    for i in (1, 2, 0):
        cols = pl.ds(512 * i, 512)
        moved = dot(put, q_i[:, cols], ((0,), (0,)))
        qkv[:, cols] = jnp.where(hit, moved, q_s[:, cols].astype(F32)).astype(BF16)
    for i in range(4):
        k_i = qkv[:, pl.ds(512 + 128 * i, 128)]
        v_i = qkv[:, pl.ds(1024 + 128 * i, 128)]
        state = dot(k_i, v_i, ((0,), (0,))).astype(BF16)
        st_s[2 * i] = state[0:64]
        st_s[2 * i + 1] = state[64:128]

    pl.semaphore_wait(barrier, 13)

    def to_z(k, src, dst, send, recv):
        zz = lax.rem(z + k, 8)
        return pltpu.make_async_remote_copy(
            src(zz), dst, send.at[k], recv.at[k],
            device_id=(y * 8 + zz, h), device_id_type=MESH,
        )

    first = [
        to_z(k, lambda zz: st_s.at[zz], st_r.at[z], sem_s, sem_r) for k in (4, 3, 5, 2, 6, 1, 7)
    ]
    for copy in first:
        copy.start()
    st_r[z] = st_s[z]

    causal = lax.broadcasted_iota(jnp.int32, (512, 512), 0) >= lax.broadcasted_iota(
        jnp.int32, (512, 512), 1
    )

    def local_attention(i):
        q_h = qkv[:, pl.ds(128 * i, 128)]
        k_h = qkv[:, pl.ds(512 + 128 * i, 128)]
        v_h = qkv[:, pl.ds(1024 + 128 * i, 128)]
        sc = jnp.where(causal, dot(q_h, k_h, ((1,), (1,))), 0.0).astype(BF16)
        att[:, pl.ds(128 * i, 128)] = dot(sc, v_h, ((1,), (0,)))

    local_attention(0)
    local_attention(1)
    for copy in first:
        copy.wait_recv()
    total = st_r[0].astype(F32)
    for k in range(1, 8):
        total = total + st_r[k].astype(F32)
    y_s[...] = total
    second = []
    for k in (2, 1, 3):
        copy = pltpu.make_async_remote_copy(
            y_s, y_r.at[y], ysem_s.at[k], ysem_r.at[k],
            device_id=(lax.rem(y + k, 4) * 8 + z, h), device_id_type=MESH,
        )
        copy.start()
        second.append(copy)
    local_attention(2)
    local_attention(3)
    y_r[y] = total
    for copy in second:
        copy.wait_recv()
    run = jnp.zeros((64, 128), F32)
    for k in range(4):
        run = run + jnp.where(k < y, y_r[k], 0.0)
    for k in range(8):
        pre_s[k] = run.astype(BF16)
        run = run + st_r[k].astype(F32)
    mine = pl.ds(pl.multiple_of(z * 64, 64), 64)
    third = [
        to_z(k, lambda zz: pre_s.at[zz], pre.at[mine], psem_s, psem_r) for k in (4, 3, 5, 2, 6, 1, 7)
    ]
    for copy in third:
        copy.start()
    pre[mine, :] = pre_s[z]
    for copy in third:
        copy.wait_recv()

    for i in range(4):
        cols = pl.ds(128 * i, 128)
        a = att[:, cols] + dot(qkv[:, cols], pre[cols, :], ((1,), (0,)))
        a = a * lax.rsqrt(jnp.mean(a * a, axis=-1, keepdims=True) + 1e-06)
        ho[:, cols] = (a * hg[:, cols]).astype(BF16)

    def chip(f):
        return lax.rem(x + s * f + 4, 4)

    def to_sib(f, m):
        rows = pl.ds(256 * m, 256)
        theirs = pl.multiple_of(chip(f) * 768 + 384 * (1 - core), 384)
        return pltpu.make_async_remote_copy(
            part.at[rows, pl.ds(theirs, 384)], sibb.at[chip(f), rows],
            bsem_s, bsem_r.at[chip(f), m], device_id=(c, sib), device_id_type=MESH,
        )

    def mixed(f, m):
        rows = pl.ds(256 * m, 256)
        cols = pl.ds(pl.multiple_of(chip(f) * 768, 768), 768)
        part[rows, cols] = dot(ho[rows, :], mix[cols, :], ((1,), (1,))).astype(BF16)
        to_sib(f, m).start()

    def on_x(n, m):
        rows = pl.ds(256 * m, 256)
        dst = chain.at[rows] if n == 0 else fin.at[n - 1, rows]
        return pltpu.make_async_remote_copy(
            pair.at[n, rows], dst, csem_s.at[n, m], csem_r.at[n, m],
            device_id=(c, xm if n == 2 else xp), device_id_type=MESH,
        )

    def paired(f, m):
        rows = pl.ds(256 * m, 256)
        to_sib(f, m).wait_recv()
        ours = pl.ds(pl.multiple_of(chip(f) * 768 + 384 * core, 384), 384)
        return part[rows, ours].astype(F32) + sibb[chip(f), rows].astype(F32)

    def send(f, m):
        rows = pl.ds(256 * m, 256)
        n = {2: 0, 1: 1, -1: 2}[f]
        value = paired(f, m)
        if n == 1:
            on_x(0, m).wait_recv()
            value = value + chain[rows, :].astype(F32)
        pair[n, rows] = value.astype(BF16)
        on_x(n, m).start()

    mixed(2, 0)
    mixed(2, 1)
    send(2, 0)
    mixed(-1, 0)
    send(2, 1)
    mixed(1, 0)
    mixed(-1, 1)
    send(-1, 0)
    mixed(1, 1)
    send(-1, 1)
    send(1, 0)
    mixed(0, 0)
    send(1, 1)
    mixed(0, 1)
    for m in range(2):
        rows = pl.ds(256 * m, 256)
        value = paired(0, m)
        on_x(2, m).wait_recv()
        value = value + fin[1, rows].astype(F32)
        on_x(1, m).wait_recv()
        out[rows, :] = (value + fin[0, rows].astype(F32)).astype(BF16)

    for copies in (first, second, third):
        for copy in copies:
            copy.wait_send()
    pltpu.make_async_remote_copy(
        sibb, sibb, bsem_s, bsem_r.at[0, 0], device_id=(c, sib), device_id_type=MESH
    ).wait_send()
    for n in range(3):
        for m in range(2):
            on_x(n, m).wait_send()


def on_device(
    enc_rows, row_counts, row_places, stream, norm_gain, proj_in, proj_out, qkv_weight, head_gain, mix_weight
):
    vmem = pl.BlockSpec(memory_space=pltpu.VMEM)
    smem = pl.BlockSpec(memory_space=pltpu.SMEM)
    hbm = pl.BlockSpec(memory_space=pl.ANY)
    dma = pltpu.SemaphoreType.DMA
    q_s, q_i, mix = pl.pallas_call(
        first_kernel,
        out_shape=(
            jax.ShapeDtypeStruct((512, 1536), BF16),
            jax.ShapeDtypeStruct((128, 1536), BF16),
            jax.ShapeDtypeStruct((3072, 512), BF16),
        ),
        in_specs=[smem, hbm, hbm, vmem, hbm, hbm, hbm, hbm],
        out_specs=(vmem, vmem, vmem),
        scratch_shapes=[
            pltpu.VMEM((1024, 768), BF16),
            pltpu.VMEM((3072, 768), BF16),
            pltpu.VMEM((3, 3072, 512), BF16),
            pltpu.VMEM((512, 3072), BF16),
            pltpu.VMEM((8, 64, 1024), BF16),
            pltpu.VMEM((128, 768), BF16),
            pltpu.VMEM((128, 3072), BF16),
            pltpu.VMEM((8, 16, 3072), BF16),
            pltpu.VMEM((128, 3072), BF16),
            dma((5,)), dma((3,)), dma((5,)), dma((5, 32)),
            dma((7,)), dma((8,)), dma((4,)), dma((8, 4)), dma((7,)), dma((8,)),
        ],
        compiler_params=pltpu.CompilerParams(
            collective_id=0, has_side_effects=True, vmem_limit_bytes=VMEM_BYTES
        ),
        name="gather_project",
    )(
        row_counts, enc_rows, stream, norm_gain.reshape(1, -1), proj_in, proj_out.T,
        mix_weight.T, qkv_weight.transpose(1, 0, 2),
    )
    return pl.pallas_call(
        second_kernel,
        out_shape=jax.ShapeDtypeStruct((512, 384), BF16),
        in_specs=[smem, vmem, vmem, vmem, vmem, vmem],
        out_specs=vmem,
        scratch_shapes=[
            pltpu.VMEM((512, 1536), BF16),
            pltpu.VMEM((8, 64, 128), BF16),
            pltpu.VMEM((8, 64, 128), BF16),
            pltpu.VMEM((64, 128), F32),
            pltpu.VMEM((4, 64, 128), F32),
            pltpu.VMEM((8, 64, 128), BF16),
            pltpu.VMEM((512, 128), BF16),
            pltpu.VMEM((512, 512), F32),
            pltpu.VMEM((512, 512), BF16),
            pltpu.VMEM((512, 3072), BF16),
            pltpu.VMEM((4, 512, 384), BF16),
            pltpu.VMEM((3, 512, 384), BF16),
            pltpu.VMEM((512, 384), BF16),
            pltpu.VMEM((2, 512, 384), BF16),
            dma((8,)), dma((8,)), dma((4,)), dma((4,)), dma((8,)), dma((8,)),
            dma, dma((4, 2)), dma((3, 2)), dma((3, 2)),
        ],
        compiler_params=pltpu.CompilerParams(
            collective_id=1, has_side_effects=True, vmem_limit_bytes=VMEM_BYTES
        ),
        name="attend_mix",
    )(row_counts, row_places, q_s, q_i, head_gain.reshape(1, -1), mix)


def solution(mesh):
    in_specs = (
        P(("ctx", "head"), None),
        P("ctx", None),
        P("ctx", None),
        P("ctx", None),
        P(),
        P("ctx", "head"),
        P("head", "ctx"),
        P(None, None, "head"),
        P("head"),
        P("head", "ctx"),
    )
    out_specs = P("ctx", "head")
    return jax.shard_map(
        on_device, mesh=mesh, in_specs=in_specs, out_specs=out_specs, check_vma=False
    )
```

```python
import heapq

import jax
import jax.numpy as jnp
from jax import lax
from jax.experimental import pallas as pl
from jax.experimental.pallas import tpu as pltpu
from jax.sharding import PartitionSpec as P

MESH = pl.DeviceIdType.MESH
BF16 = jnp.bfloat16
F32 = jnp.float32
VMEM_BYTES = 64 * 1024 * 1024 - 65536

PIECES = (
    (0, "A", 0, 32, 32, 1536),
    (1, "z", 0, 48, 96, 1536),
    (1, "z", 48, 48, 96, 1536),
    (2, "a", 0, 64, 96, 1024),
    (2, "b", 64, 32, 96, 1024),
)
CHUNKS = (31, 7, 7, 31, 31)
MIX = 3


def forwards(tree, dy, dz):
    out = []
    along_z = []
    if -4 < dz <= 0:
        along_z.append(("z+", (dy, dz - 1)))
    if 0 <= dz < 3:
        along_z.append(("z-", (dy, dz + 1)))
    if tree == "z":
        return along_z
    if tree in "aA":
        if tree == "A":
            along_z = {
                -2: [("z+", (0, -3)), ("zz+", (0, -4))],
                0: [("z+", (0, -1)), ("z-", (0, 1)), ("zz+", (0, -2)), ("zz-", (0, 2))],
                2: [("z-", (0, 3))],
            }.get(dz, [])
        if dy == 0:
            out += along_z + [("y+", (-1, dz)), ("y-", (1, dz))]
        elif dy == -1 and dz % 2 == 0:
            out.append(("y+", (-2, dz)))
        elif dy == 1 and dz % 2 != 0:
            out.append(("y-", (-2, dz)))
    else:
        if dz == 0:
            if dy == 0:
                out += [("y+", (-1, 0)), ("y-", (1, 0))]
            elif dy == -1:
                out.append(("y+", (-2, 0)))
        out += along_z
    return out


def plan():
    rate, hop = 46.5e3, 2.3
    free = dict.fromkeys(("z+", "z-", "y+", "y-"), 0.0)
    now, order, heap = 0.0, [], []
    released, left = set(), list(CHUNKS)
    tasks = [(("norm", i), 0.2) for i in range(8)] + [(("stream", i), 0.9) for i in range(12)]
    tasks.insert(16, (("put",), 0.4))
    near_z, all_z, urgent, fan_left, fanned, gathered = 2, 7, False, 7, False, False
    hid_done, waiting, ready, parts, summed = False, {-1: 2, 1: 2, -2: 2}, [], 0, 0
    for at, name in ((6.5, "enc1"), (11.0, "enc2"), (14.0, "enc3")):
        heapq.heappush(heap, (at, (name,)))

    def later(delay, *event):
        heapq.heappush(heap, (now + delay, event))

    def travel(link, size, *event):
        if link[:2] == "zz":
            link, size = link[1:], 2 * size
        free[link] = max(free[link], now) + size / rate
        slack = 0.5 if event[0] == "rx" and event[1] >= MIX else 0.0
        heapq.heappush(heap, (free[link] + hop + slack, event))

    def issue(p, dy, dz):
        _, tree, _, rows, _, width = PIECES[p]
        for link, target in forwards(tree, dy, dz):
            if p == MIX and dy == 0 and link[0] == "y" and not fanned:
                continue
            travel(link, rows * width, "rx", p, *target)

    while True:
        for p in range(len(PIECES)):
            open_now = p == 0 or (near_z == 0 if p < MIX else sum(left[1:MIX]) == 0)
            if p not in released and open_now:
                released.add(p)
                order.append(("own", p))
                issue(p, 0, 0)
        if gathered and fan_left == 0 and not fanned:
            fanned = True
            order.append(("fan",))
            for dz in (0, -1, 1, -2, 2, -3, 3, -4):
                for link, target in forwards("a", 0, dz):
                    if link[0] == "y":
                        travel(link, PIECES[MIX][3] * PIECES[MIX][5], "rx", MIX, *target)
        if heap and heap[0][0] <= now:
            event = heapq.heappop(heap)[1]
            order.append(event)
            kind = event[0]
            if kind == "rx":
                _, p, dy, dz = event
                left[p] -= 1
                fan_left -= p == MIX and dy == 0
                near_z -= p == 0 and dy == 0 and abs(dz) == 2
                all_z -= p == 0 and dy == 0
                issue(p, dy, dz)
            elif kind == "hy":
                _, dy, q = event
                if dy == -1 and q == 0:
                    travel("y+", 98304, "hy", -2, 0)
                elif dy == 1 and q == 1:
                    travel("y-", 98304, "hy", -2, 1)
                waiting[dy] -= 1
                if waiting[dy] == 0:
                    ready.append(dy)
            elif kind == "rs":
                now += 0.2
                summed += 1
                if summed == 4:
                    later(3.2, "yi")
            elif kind == "yi":
                now += 0.4
                gathered = True
                for g in range(2):
                    later(3.2 + g, "ag1", g)
                    later(5.5 + g, "ag2", g)
                    later(6.8 + g, "ag3", g)
            elif kind == "ag3" and event[1] == 1:
                tasks += [(("image", 1), 0.7), (("image", 2), 0.7), (("state",), 1.0), (("image", 0), 0.9)]
                urgent = True
            elif kind == "z1":
                now += 0.3
                later(3.2, "y1")
            elif kind == "y1":
                now += 0.4
                later(5.0, "z2")
            continue
        if left[0] == 0 and not hid_done and ("enc3",) in order:
            order.append(("hid",))
            hid_done = True
            now += 1.3
            for q in (0, 1):
                travel("y+", 98304, "hy", -1, q)
                travel("y-", 98304, "hy", 1, 1 - q)
            ready.append(0)
            continue
        if ready and sum(left[1:MIX]) == 0:
            dy = ready.pop(0)
            order.append(("part", dy))
            now += 0.5
            later(3.0, "rs", dy)
            continue
        if tasks and (
            urgent or not heap or heap[0][0] >= now + 0.7 * tasks[0][1]
        ) and (all_z == 0 or tasks[0][0][0] == "norm"):
            task, time = tasks.pop(0)
            order.append(task)
            now += time
            if task == ("state",):
                later(5.0, "z1")
            elif task == ("image", 0):
                tasks += [(("local", i), 0.55) for i in range(4)]
            continue
        if not heap:
            return order
        now = max(now, heap[0][0])


ORDER = plan()


def dot(a, b, dims):
    return lax.dot_general(a, b, (dims, ((), ())), preferred_element_type=F32)


def silu(v):
    return v * jax.nn.sigmoid(v)


def live_slots(counts_ref):
    slot = lax.broadcasted_iota(jnp.int32, (8, 512), 1)
    rank = jnp.full((8, 512), -1, jnp.int32)
    before = jnp.int32(0)
    for h in range(8):
        count = counts_ref[0, h]
        within = slot - 64 * h
        mine = (within >= 0) & (within < 64) & (within < count)
        rank = jnp.where(mine, within + before, rank)
        before = before + count
    return rank


def place_of_me():
    c, h = lax.axis_index("ctx"), lax.axis_index("head")
    y, z, x, core = c // 8, c % 8, h // 2, h % 2
    return c, h, y, z, x, core, 1 - 2 * core


def kernel(
    counts, places, hg, enc, stream, gain, a_in, b_in, c_in, w_in,
    out,
    buf_a, buf_b, mix, wq, xs, encb, hidb, pbuf, rbuf, isum, ibuf, nbuf, q_i, put, hit,
    qkv, st_s, st_r, y_s, y_r, pre_s, pre, att, ho, part, sibb, pair, chain, fin,
    lsem, wsem, ssem, rsem, es, er, hs, hr, ps, pr, ts, tr, gs, gr,
    sem_s, sem_r, ysem_s, ysem_r, psem_s, psem_r, bsem_s, bsem_r, csem_s, csem_r,
):
    c, h, y, z, x, core, s = place_of_me()
    bufs = (buf_a, buf_b, mix)
    own = []
    bases = (c * 32, z * 96, c * 96)
    for i, (src, buf, rows) in enumerate(((a_in, buf_a, 32), (b_in, buf_b, 96), (c_in, mix, 96))):
        own.append(
            pltpu.make_async_copy(src, buf.at[pl.ds(pl.multiple_of(bases[i], 32), rows)], lsem.at[i])
        )
    load_x = pltpu.make_async_copy(stream, xs, lsem.at[3])
    own.append(pltpu.make_async_copy(enc, encb.at[h], lsem.at[4]))
    load_w = [pltpu.make_async_copy(w_in.at[i], wq.at[i], wsem.at[i]) for i in range(3)]
    for copy in own:
        copy.start()
    load_x.start()
    load_w[0].start()

    def y_at(dy):
        return lax.rem(y + s * dy + 8, 4)

    def z_at(dz):
        return lax.rem(z + s * dz + 16, 8)

    links = {
        "z+": y * 8 + z_at(1), "z-": y * 8 + z_at(-1), "y+": y_at(1) * 8 + z, "y-": y_at(-1) * 8 + z,
        "zz+": y * 8 + z_at(2), "zz-": y * 8 + z_at(-2),
    }
    sib = 2 * x + 1 - core
    xp = 2 * lax.rem(x + s + 4, 4) + core
    xm = 2 * lax.rem(x - s + 4, 4) + core
    xd = 2 * lax.rem(x + 2, 4) + core

    barrier = pltpu.get_barrier_semaphore()
    for k in range(1, 8):
        pl.semaphore_signal(
            barrier, inc=1, device_id=(y * 8 + lax.rem(z + k, 8), h), device_id_type=MESH
        )
        pl.semaphore_signal(
            barrier, inc=1, device_id=(c, lax.rem(h + k, 8)), device_id_type=MESH
        )
    for k in range(1, 4):
        pl.semaphore_signal(
            barrier, inc=1, device_id=(lax.rem(y + k, 4) * 8 + z, h), device_id_type=MESH
        )
    pl.semaphore_wait(barrier, 17)
    for copy in own:
        copy.wait()

    def remote(src, dst, send, recv, to):
        return pltpu.make_async_remote_copy(
            src, dst, send, recv, device_id=to, device_id_type=MESH
        )

    def chunk(p, dy, dz):
        b, _, first, rows, shard, _ = PIECES[p]
        position = z_at(dz) if b == 1 else y_at(dy) * 8 + z_at(dz)
        row = pl.multiple_of(position * shard + first, 16)
        return bufs[b].at[pl.ds(row, rows)]

    def index(dy, dz):
        return (dy + 2) * 8 + dz + 4

    def spread(p, dy, dz, only="zy"):
        ref = chunk(p, dy, dz)
        if p == MIX and dy == 0 and only == "zy":
            only = "z"
        for link, target in forwards(PIECES[p][1], dy, dz):
            if link[0] not in only:
                continue
            remote(ref, ref, ssem.at[p], rsem.at[p, index(*target)], (links[link], h)).start()

    def arrived(p, dy, dz):
        ref = chunk(p, dy, dz)
        remote(ref, ref, ssem.at[p], rsem.at[p, index(dy, dz)], (links["z+"], h)).wait_recv()

    def over_head(refs, sends, recvs):
        def push(owner, to, n, slot):
            remote(refs(owner), refs(owner), sends(n), recvs(slot), (c, to)).start()

        def take(owner, slot):
            remote(refs(owner), refs(owner), sends(0), recvs(slot), (c, sib)).wait_recv()

        def begin():
            push(h, xp, 0, 1)
            push(h, xm, 1, 2)
            push(h, sib, 2, 4)

        def one():
            take(xm, 1)
            push(xm, xp, 3, 3)
            push(xm, sib, 4, 5)
            take(xp, 2)
            push(xp, sib, 5, 6)

        def two():
            take(xd, 3)
            push(xd, sib, 6, 7)

        def three():
            for slot in (4, 5, 6, 7):
                take(sib, slot)

        def drain():
            for n in range(7):
                remote(refs(h), refs(h), sends(n), recvs(0), (c, sib)).wait_send()

        return begin, one, two, three, drain

    enc_steps = over_head(lambda o: encb.at[o], lambda n: es.at[n], lambda n: er.at[n])
    ag_steps = [
        over_head(
            lambda o, g=g: nbuf.at[pl.ds(pl.multiple_of(o * 16, 16), 16), pl.ds(1536 * g, 1536)],
            lambda n, g=g: gs.at[g, n],
            lambda n, g=g: gr.at[g, n],
        )
        for g in range(2)
    ]
    enc_steps[0]()

    def norm(v):
        return v * lax.rsqrt(jnp.mean(v * v, axis=-1, keepdims=True) + 1e-05) * gain[...]

    def hid_ref(dy, q):
        return hidb.at[y_at(dy), pl.ds(64 * q, 64)]

    def hid_send(dy, q, n, link, at):
        slot = {-1: 0, 1: 1, -2: 2}[at]
        return remote(hid_ref(dy, q), hid_ref(dy, q), hs.at[n], hr.at[slot, q], (links[link], h))

    def placed(i):
        cols = pl.ds(512 * i, 512)
        moved = dot(put[...], q_i[:, cols], ((0,), (0,)))
        qkv[:, cols] = jnp.where(
            hit[:, 0:1] > 0.5, moved, qkv[:, cols].astype(F32)
        ).astype(BF16)

    def to_z(k, src, dst, send, recv):
        zz = lax.rem(z + k, 8)
        return remote(src.at[zz], dst, send.at[k], recv.at[k], (y * 8 + zz, h))

    far_first = (4, 3, 5, 2, 6, 1, 7)
    mine_z = pl.ds(pl.multiple_of(z * 64, 64), 64)
    z_first = [to_z(k, st_s, st_r.at[z], sem_s, sem_r) for k in far_first]
    z_last = [to_z(k, pre_s, pre.at[mine_z], psem_s, psem_r) for k in far_first]
    y_sums = [
        remote(y_s, y_r.at[y], ysem_s.at[k], ysem_r.at[k], (lax.rem(y + k, 4) * 8 + z, h))
        for k in (2, 1, 3)
    ]

    for event in ORDER:
        kind = event[0]
        if kind == "own":
            spread(event[1], 0, 0)
        elif kind == "rx":
            arrived(*event[1:])
            spread(*event[1:])
        elif kind == "fan":
            for dz in (0, -1, 1, -2, 2, -3, 3, -4):
                spread(MIX, 0, dz, "y")
        elif kind == "norm":
            if event[1] == 0:
                load_x.wait()
            rows = pl.ds(64 * event[1], 64)
            xs[rows, :] = norm(xs[rows, :].astype(F32)).astype(BF16)
        elif kind == "stream":
            i, part_of = divmod(event[1], 4)
            if part_of == 0:
                load_w[i].wait()
                if i < 2:
                    load_w[i + 1].start()
            half, low = divmod(part_of, 2)
            rows = pl.ds(256 * low, 256)
            value = silu(dot(xs[rows, :], wq[i, :, pl.ds(256 * half, 256)], ((1,), (0,))))
            qkv[rows, pl.ds(512 * i + 256 * half, 256)] = value.astype(BF16)
        elif kind == "put":
            rank = live_slots(counts)[0:1, :]
            row = lax.broadcasted_iota(jnp.int32, (128, 512), 0)
            local = places[...] - c * 512
            where = jnp.sum(jnp.where(row == rank, local, 0).astype(F32), axis=1, keepdims=True)
            token = lax.broadcasted_iota(jnp.int32, (128, 512), 1)
            put[...] = jnp.where(token == where.astype(jnp.int32), 1.0, 0.0).astype(BF16)
            hit[...] = dot(put[...], jnp.ones((128, 128), BF16), ((0,), (0,)))
        elif kind == "hid":
            rank = live_slots(counts)
            row = lax.broadcasted_iota(jnp.int32, (128, 512), 0)
            pick = jnp.where(row == rank[0:1, :], 1.0, 0.0).astype(BF16)
            rows = dot(pick, encb[...].reshape(512, 1024), ((1,), (0,))).astype(BF16)
            u = dot(rows, buf_a[...], ((1,), (0,)))
            hidb[y] = (0.5 * u * (1.0 + lax.erf(u * 0.7071067811865476))).astype(BF16)
            hid_send(0, 0, 0, "y+", -1).start()
            hid_send(0, 1, 1, "y-", 1).start()
            hid_send(0, 1, 2, "y+", -1).start()
            hid_send(0, 0, 3, "y-", 1).start()
        elif kind == "hy":
            dy, q = event[1:]
            hid_send(dy, q, 0, "y+", dy).wait_recv()
            if dy == -1 and q == 0:
                hid_send(-1, 0, 4, "y+", -2).start()
            elif dy == 1 and q == 1:
                hid_send(1, 1, 5, "y-", -2).start()
        elif kind == "part":
            yy = y_at(event[1])
            pbuf[yy] = dot(hidb[yy], buf_b[...], ((1,), (1,))).astype(BF16)
            for k in range(1, 8):
                to = lax.rem(h + k, 8)
                remote(
                    pbuf.at[yy, pl.ds(pl.multiple_of(to * 16, 16), 16)],
                    rbuf.at[h, yy], ps.at[event[1] + 2], pr.at[h, yy], (c, to),
                ).start()
        elif kind == "rs":
            yy = y_at(event[1])
            total = pbuf[yy, pl.ds(pl.multiple_of(h * 16, 16), 16), :].astype(F32)
            for k in range(1, 8):
                frm = lax.rem(h + k, 8)
                ref = rbuf.at[frm, yy]
                remote(ref, ref, ps.at[0], pr.at[frm, yy], (c, frm)).wait_recv()
                total = total + rbuf[frm, yy].astype(F32)
            here = pl.ds(pl.multiple_of(y * 768, 768), 768)
            if event[1] == 0:
                ibuf[:, here] = total.astype(BF16)
            else:
                isum[yy] = total.astype(BF16)
                remote(
                    isum.at[yy], ibuf.at[:, here], ts.at[event[1] + 2], tr.at[y], (yy * 8 + z, h)
                ).start()
        elif kind == "yi":
            for k in range(1, 4):
                yy = lax.rem(y + k, 4)
                there = pl.ds(pl.multiple_of(yy * 768, 768), 768)
                remote(
                    isum.at[yy], ibuf.at[:, there], ts.at[0], tr.at[yy], (yy * 8 + z, h)
                ).wait_recv()
            mine = pl.ds(pl.multiple_of(h * 16, 16), 16)
            nbuf[mine, :] = norm(ibuf[...].astype(F32)).astype(BF16)
            for g in range(2):
                ag_steps[g][0]()
        elif kind in ("ag1", "ag2", "ag3"):
            ag_steps[event[1]][int(kind[2])]()
        elif kind in ("enc1", "enc2", "enc3"):
            enc_steps[int(kind[3])]()
        elif kind == "image":
            i = event[1]
            value = silu(dot(nbuf[...], wq[i], ((1,), (0,))))
            q_i[:, pl.ds(512 * i, 512)] = value.astype(BF16)
            if i == 0:
                placed(0)
        elif kind == "state":
            placed(1)
            placed(2)
            for i in range(4):
                k_i = qkv[:, pl.ds(512 + 128 * i, 128)]
                v_i = qkv[:, pl.ds(1024 + 128 * i, 128)]
                state = dot(k_i, v_i, ((0,), (0,))).astype(BF16)
                st_s[2 * i] = state[0:64]
                st_s[2 * i + 1] = state[64:128]
            for copy in z_first:
                copy.start()
            st_r[z] = st_s[z]
        elif kind == "local":
            i = event[1]
            causal = lax.broadcasted_iota(jnp.int32, (512, 512), 0) >= lax.broadcasted_iota(
                jnp.int32, (512, 512), 1
            )
            q_h = qkv[:, pl.ds(128 * i, 128)]
            k_h = qkv[:, pl.ds(512 + 128 * i, 128)]
            v_h = qkv[:, pl.ds(1024 + 128 * i, 128)]
            sc = jnp.where(causal, dot(q_h, k_h, ((1,), (1,))), 0.0).astype(BF16)
            att[:, pl.ds(128 * i, 128)] = dot(sc, v_h, ((1,), (0,)))
        elif kind == "z1":
            for copy in z_first:
                copy.wait_recv()
            total = st_r[0].astype(F32)
            for k in range(1, 8):
                total = total + st_r[k].astype(F32)
            y_s[...] = total.astype(BF16)
            for copy in y_sums:
                copy.start()
            y_r[y] = y_s[...]
        elif kind == "y1":
            for copy in y_sums:
                copy.wait_recv()
            run = jnp.zeros((64, 128), F32)
            for k in range(4):
                run = run + jnp.where(k < y, y_r[k].astype(F32), 0.0)
            for k in range(8):
                pre_s[k] = run.astype(BF16)
                run = run + st_r[k].astype(F32)
            for copy in z_last:
                copy.start()
            pre[mine_z, :] = pre_s[z]
        elif kind == "z2":
            for copy in z_last:
                copy.wait_recv()

    for i in range(4):
        cols = pl.ds(128 * i, 128)
        a = att[:, cols] + dot(qkv[:, cols], pre[cols, :], ((1,), (0,)))
        a = a * lax.rsqrt(jnp.mean(a * a, axis=-1, keepdims=True) + 1e-06)
        ho[:, cols] = (a * hg[:, cols]).astype(BF16)

    def chip(f):
        return lax.rem(x + s * f + 4, 4)

    def to_sib(f, m):
        rows = pl.ds(256 * m, 256)
        theirs = pl.multiple_of(chip(f) * 768 + 384 * (1 - core), 384)
        return pltpu.make_async_remote_copy(
            part.at[rows, pl.ds(theirs, 384)], sibb.at[chip(f), rows],
            bsem_s, bsem_r.at[chip(f), m], device_id=(c, sib), device_id_type=MESH,
        )

    def mixed(f, m):
        rows = pl.ds(256 * m, 256)
        cols = pl.ds(pl.multiple_of(chip(f) * 768, 768), 768)
        part[rows, cols] = dot(ho[rows, :], mix[cols, :], ((1,), (1,))).astype(BF16)
        to_sib(f, m).start()

    def on_x(n, m):
        rows = pl.ds(256 * m, 256)
        dst = chain.at[rows] if n == 0 else fin.at[n - 1, rows]
        return pltpu.make_async_remote_copy(
            pair.at[n, rows], dst, csem_s.at[n, m], csem_r.at[n, m],
            device_id=(c, xm if n == 2 else xp), device_id_type=MESH,
        )

    def paired(f, m):
        rows = pl.ds(256 * m, 256)
        to_sib(f, m).wait_recv()
        ours = pl.ds(pl.multiple_of(chip(f) * 768 + 384 * core, 384), 384)
        return part[rows, ours].astype(F32) + sibb[chip(f), rows].astype(F32)

    def send(f, m):
        rows = pl.ds(256 * m, 256)
        n = {2: 0, 1: 1, -1: 2}[f]
        value = paired(f, m)
        if n == 1:
            on_x(0, m).wait_recv()
            value = value + chain[rows, :].astype(F32)
        pair[n, rows] = value.astype(BF16)
        on_x(n, m).start()

    mixed(2, 0)
    mixed(2, 1)
    send(2, 0)
    mixed(-1, 0)
    send(2, 1)
    mixed(1, 0)
    mixed(-1, 1)
    send(-1, 0)
    mixed(1, 1)
    send(-1, 1)
    send(1, 0)
    mixed(0, 0)
    send(1, 1)
    mixed(0, 1)
    for m in range(2):
        rows = pl.ds(256 * m, 256)
        value = paired(0, m)
        on_x(2, m).wait_recv()
        value = value + fin[1, rows].astype(F32)
        on_x(1, m).wait_recv()
        out[rows, :] = (value + fin[0, rows].astype(F32)).astype(BF16)

    for copies in (z_first, y_sums, z_last):
        for copy in copies:
            copy.wait_send()
    remote(sibb, sibb, bsem_s, bsem_r.at[0, 0], (c, sib)).wait_send()
    for n in range(3):
        for m in range(2):
            on_x(n, m).wait_send()
    for p, (b, _, _, rows, _, _) in enumerate(PIECES):
        ref = bufs[b].at[pl.ds(0, CHUNKS[p] * rows)]
        remote(ref, ref, ssem.at[p], rsem.at[p, 0], (links["z+"], h)).wait_send()
    for n in range(6):
        remote(hid_ref(0, 0), hid_ref(0, 0), hs.at[n], hr.at[0, 0], (links["y+"], h)).wait_send()
    for f in range(4):
        ref = pbuf.at[0, pl.ds(0, 112)]
        remote(ref, ref, ps.at[f], pr.at[0, 0], (c, sib)).wait_send()
        if f != 2:
            ref = isum.at[0]
            remote(ref, ref, ts.at[f], tr.at[0], (links["y+"], h)).wait_send()
    enc_steps[4]()
    for g in range(2):
        ag_steps[g][4]()


def on_device(
    enc_rows, row_counts, row_places, stream, norm_gain, proj_in, proj_out, qkv_weight, head_gain, mix_weight
):
    vmem = pl.BlockSpec(memory_space=pltpu.VMEM)
    smem = pl.BlockSpec(memory_space=pltpu.SMEM)
    hbm = pl.BlockSpec(memory_space=pl.ANY)
    dma = pltpu.SemaphoreType.DMA

    def b16(*shape):
        return pltpu.VMEM(shape, BF16)

    def f32(*shape):
        return pltpu.VMEM(shape, F32)

    return pl.pallas_call(
        kernel,
        out_shape=jax.ShapeDtypeStruct((512, 384), BF16),
        in_specs=[smem, vmem, vmem, hbm, hbm, vmem, hbm, hbm, hbm, hbm],
        out_specs=vmem,
        scratch_shapes=[
            b16(1024, 768), b16(768, 768), b16(3072, 512), b16(3, 3072, 512), b16(512, 3072),
            b16(8, 64, 1024), b16(4, 128, 768), b16(4, 128, 768), b16(8, 4, 16, 768),
            b16(4, 16, 768), b16(16, 3072), b16(128, 3072), b16(128, 1536), b16(128, 512),
            f32(512, 128),
            b16(512, 1536), b16(8, 64, 128), b16(8, 64, 128), b16(64, 128), b16(4, 64, 128),
            b16(8, 64, 128), b16(512, 128), f32(512, 512), b16(512, 512), b16(512, 3072),
            b16(4, 512, 384), b16(3, 512, 384), b16(512, 384), b16(2, 512, 384),
            dma((5,)), dma((3,)), dma((6,)), dma((6, 32)), dma((7,)), dma((8,)),
            dma((6,)), dma((3, 2)), dma((4,)), dma((8, 4)), dma((4,)), dma((4,)),
            dma((2, 7)), dma((2, 8)),
            dma((8,)), dma((8,)), dma((4,)), dma((4,)), dma((8,)), dma((8,)),
            dma, dma((4, 2)), dma((3, 2)), dma((3, 2)),
        ],
        compiler_params=pltpu.CompilerParams(
            collective_id=0, has_side_effects=True, vmem_limit_bytes=VMEM_BYTES
        ),
        name="project_attend_mix",
    )(
        row_counts, row_places, head_gain.reshape(1, -1), enc_rows, stream,
        norm_gain.reshape(1, -1), proj_in, proj_out.T, mix_weight.T, qkv_weight.transpose(1, 0, 2),
    )


def solution(mesh):
    in_specs = (
        P(("ctx", "head"), None),
        P("ctx", None),
        P("ctx", None),
        P("ctx", None),
        P(),
        P("ctx", "head"),
        P("head", "ctx"),
        P(None, None, "head"),
        P("head"),
        P("head", "ctx"),
    )
    out_specs = P("ctx", "head")
    return jax.shard_map(
        on_device, mesh=mesh, in_specs=in_specs, out_specs=out_specs, check_vma=False
    )
```

```python
import heapq

import jax
import jax.numpy as jnp
from jax import lax
from jax.experimental import pallas as pl
from jax.experimental.pallas import tpu as pltpu
from jax.sharding import PartitionSpec as P

MESH = pl.DeviceIdType.MESH
BF16 = jnp.bfloat16
F32 = jnp.float32
VMEM_BYTES = 64 * 1024 * 1024 - 65536

PIECES = (
    (0, "A", 0, 32, 32, 0, 384),
    (0, "A", 0, 32, 32, 384, 384),
    (1, "z", 0, 32, 96, 0, 768),
    (1, "z", 32, 32, 96, 0, 768),
    (1, "z", 64, 32, 96, 0, 768),
    (2, "A", 0, 64, 96, 0, 512),
    (2, "b", 64, 32, 96, 0, 512),
)
CHUNKS = (31, 31, 7, 7, 7, 31, 31)
RELEASE = (0, 0, 4, 4, 4, 83, 83)
MIX = 5
SLACK = 1.5
EARLY, LATE = 0.4, 0.9


def forwards(tree, dy, dz):
    out = []
    along_z = []
    if -4 < dz <= 0:
        along_z.append(("z+", (dy, dz - 1)))
    if 0 <= dz < 3:
        along_z.append(("z-", (dy, dz + 1)))
    if tree == "z":
        return along_z
    if tree in "aA":
        if tree == "A":
            along_z = {
                -2: [("z+", (0, -3)), ("zz+", (0, -4))],
                0: [("z+", (0, -1)), ("z-", (0, 1)), ("zz+", (0, -2)), ("zz-", (0, 2))],
                2: [("z-", (0, 3))],
            }.get(dz, [])
        if dy == 0:
            out += along_z + [("y+", (-1, dz)), ("y-", (1, dz))]
        elif dy == -1 and dz % 2 == 0:
            out.append(("y+", (-2, dz)))
        elif dy == 1 and dz % 2 != 0:
            out.append(("y-", (-2, dz)))
    else:
        if dz == 0:
            if dy == 0:
                out += [("y+", (-1, 0)), ("y-", (1, 0))]
            elif dy == -1:
                out.append(("y+", (-2, 0)))
        out += along_z
    return out


def ends(tree):
    out = []
    for dy in ((0,) if tree == "z" else (-2, -1, 0, 1)):
        for dz in range(-4, 4):
            if (dy, dz) != (0, 0) and not forwards(tree, dy, dz):
                out.append((dy, dz))
    return out


def semaphores():
    places, total = [], 0
    for _, tree, *_ in PIECES:
        last = ends(tree)
        place = dict.fromkeys(last, total)
        total += 1
        for dy in ((0,) if tree == "z" else (-2, -1, 0, 1)):
            for dz in range(-4, 4):
                if (dy, dz) != (0, 0) and (dy, dz) not in place:
                    place[dy, dz] = total
                    total += 1
        places.append(place)
    return places, total


def plan():
    rate, hop = 46.5e3, 2.3
    free = dict.fromkeys(("z+", "z-", "y+", "y-", "x"), 0.0)
    now, count, order, heap = 0.0, 0, [], []
    released, left = set(), list(CHUNKS)
    tasks = [(("norm", i), 0.2) for i in range(8)] + [(("stream", i), 1.0) for i in range(12)]
    tasks.insert(16, (("put",), 0.4))
    near_z, fan_left, fanned, gathered, urgent = 7, 7, False, False, False
    last = [ends(piece[1]) for piece in PIECES]
    open_ends = [len(e) for e in last]
    hids, waiting, ready, summed = 0, {0: 2, -1: 2, 1: 2, -2: 2}, [], 0
    for at, name in ((7.5, "enc1"), (11.0, "enc2"), (14.0, "enc3")):
        heapq.heappush(heap, (at, (name,)))

    def later(delay, *event):
        heapq.heappush(heap, (now + delay, event))

    def travel(link, size, *event):
        if link[:2] == "zz":
            link, size = link[1:], 2 * size
        free[link] = max(free[link], now) + size / rate
        first = 1.8 if now < 1.0 else 0.0
        slack = SLACK if event[0] == "rx" and event[1] >= MIX else 0.0
        heapq.heappush(heap, (free[link] + hop + first + slack, event))

    def size_of(p):
        return PIECES[p][3] * PIECES[p][6] * 2

    def issue(p, dy, dz):
        for link, target in forwards(PIECES[p][1], dy, dz):
            if p == MIX and dy == 0 and link[0] == "y" and not fanned:
                continue
            travel(link, size_of(p), "rx", p, *target)

    while True:
        for p in range(len(PIECES)):
            if p not in released and count >= RELEASE[p]:
                released.add(p)
                order.append(("own", p))
                issue(p, 0, 0)
        if gathered and fan_left == 0 and not fanned:
            fanned = True
            order.append(("fan",))
            for dz in (0, -1, 1, -2, 2, -3, 3, -4):
                for link, target in forwards("a", 0, dz):
                    if link[0] == "y":
                        travel(link, size_of(MIX), "rx", MIX, *target)
        if heap and heap[0][0] <= now:
            event = heapq.heappop(heap)[1]
            kind = event[0]
            if kind == "rx" and event[2:] in last[event[1]]:
                p = event[1]
                count += 1
                left[p] -= 1
                open_ends[p] -= 1
                fan_left -= p == MIX and event[2] == 0
                near_z -= p == 0 and event[2] == 0
                if open_ends[p] == 0:
                    order.append(("ends", p))
                continue
            order.append(event)
            if kind == "rx":
                _, p, dy, dz = event
                count += 1
                left[p] -= 1
                fan_left -= p == MIX and dy == 0
                near_z -= p == 0 and dy == 0
                issue(p, dy, dz)
            elif kind == "hy":
                _, dy, q = event
                if dy == -1 and q == 0:
                    travel("y+", 98304, "hy", -2, 0)
                elif dy == 1 and q == 1:
                    travel("y-", 98304, "hy", -2, 1)
                waiting[dy] -= 1
                if waiting[dy] == 0:
                    ready.append(dy)
            elif kind == "rs":
                now += 0.1
                summed += 1
                if summed == 4:
                    later(3.6, "yi")
            elif kind == "yi":
                now += 0.4
                gathered = True
                for g in range(2):
                    later(3.6 + g, "ag1", g)
                    later(6.2 + g, "ag2", g)
                    later(7.4 + g, "ag3", g)
            elif kind == "ag3" and event[1] == 1:
                tasks += [(("image", 1), 0.7), (("image", 2), 0.7), (("state",), 1.0), (("image", 0), 0.9)]
                urgent = True
            elif kind == "z1":
                now += 0.1
                later(3.6, "y1")
            elif kind == "y1":
                now += 0.4
                later(5.2, "z2")
            continue
        if hids < 2 and left[hids] == 0 and ("enc3",) in order:
            order.append(("hid", hids))
            now += 0.6 if hids == 0 else 0.4
            travel("y+", 98304, "hy", -1, hids)
            travel("y-", 98304, "hy", 1, hids)
            hids += 1
            if hids == 2:
                ready.append(0)
            continue
        if ready and sum(left[2:MIX]) == 0:
            dy = ready.pop(0)
            order.append(("part", dy))
            now += 0.65
            travel("x", 98304, "rs", dy)
            continue
        if tasks and (
            urgent or not heap or heap[0][0] >= now + (LATE if hids == 2 else EARLY) * tasks[0][1]
        ) and (near_z == 0 or tasks[0][0][0] == "norm"):
            task, time = tasks.pop(0)
            order.append(task)
            now += time
            if task == ("state",):
                later(5.0, "z1")
            elif task == ("image", 0):
                tasks += [(("local", i), 0.55) for i in range(4)]
            continue
        if not heap:
            return order
        now = max(now, heap[0][0])


ORDER = plan()
PLACES, ARRIVALS = semaphores()


def dot(a, b, dims):
    return lax.dot_general(a, b, (dims, ((), ())), preferred_element_type=F32)


def silu(v):
    return v * jax.nn.sigmoid(v)


def live_slots(counts_ref):
    slot = lax.broadcasted_iota(jnp.int32, (8, 512), 1)
    rank = jnp.full((8, 512), -1, jnp.int32)
    before = jnp.int32(0)
    for h in range(8):
        count = counts_ref[0, h]
        within = slot - 64 * h
        mine = (within >= 0) & (within < 64) & (within < count)
        rank = jnp.where(mine, within + before, rank)
        before = before + count
    return rank


def place_of_me():
    c, h = lax.axis_index("ctx"), lax.axis_index("head")
    y, z, x, core = c // 8, c % 8, h // 2, h % 2
    return c, h, y, z, x, core, 1 - 2 * core


def kernel(
    counts, places, hg, enc, stream, gain, a_in, b_in, c_in, w_in,
    out,
    buf_a, buf_b, mix, wq, xs, encb, rows_i, hidb, pbuf, rbuf, isum, ibuf, nbuf, q_i, put, hit,
    qkv, st_s, st_r, y_s, y_r, pre_s, pre, att, ho, part, sibb, pair, chain, fin,
    lsem, wsem, ssem, rsem, es, er, hs, hr, ps, pr, ts, tr, gs, gr,
    sem_s, sem_r, ysem_s, ysem_r, psem_s, psem_r, bsem_s, bsem_r, csem_s, csem_r,
):
    c, h, y, z, x, core, s = place_of_me()
    bufs = (buf_a, buf_b, mix)
    own = []
    bases = (c * 32, z * 96, c * 96)
    for i, (src, buf, rows) in enumerate(((a_in, buf_a, 32), (b_in, buf_b, 96), (c_in, mix, 96))):
        own.append(
            pltpu.make_async_copy(src, buf.at[pl.ds(pl.multiple_of(bases[i], 32), rows)], lsem.at[i])
        )
    load_x = pltpu.make_async_copy(stream, xs, lsem.at[3])
    own.append(pltpu.make_async_copy(enc, encb.at[h], lsem.at[4]))
    load_w = [pltpu.make_async_copy(w_in.at[i], wq.at[i], wsem.at[i]) for i in range(3)]
    for copy in own:
        copy.start()
    load_x.start()
    load_w[0].start()

    def y_at(dy):
        return lax.rem(y + s * dy + 8, 4)

    def z_at(dz):
        return lax.rem(z + s * dz + 16, 8)

    links = {
        "z+": y * 8 + z_at(1), "z-": y * 8 + z_at(-1), "y+": y_at(1) * 8 + z, "y-": y_at(-1) * 8 + z,
        "zz+": y * 8 + z_at(2), "zz-": y * 8 + z_at(-2),
    }
    sib = 2 * x + 1 - core
    xp = 2 * lax.rem(x + s + 4, 4) + core
    xm = 2 * lax.rem(x - s + 4, 4) + core
    xd = 2 * lax.rem(x + 2, 4) + core

    barrier = pltpu.get_barrier_semaphore()
    for k in range(1, 8):
        pl.semaphore_signal(
            barrier, inc=1, device_id=(y * 8 + lax.rem(z + k, 8), h), device_id_type=MESH
        )
        pl.semaphore_signal(
            barrier, inc=1, device_id=(c, lax.rem(h + k, 8)), device_id_type=MESH
        )
    for k in range(1, 4):
        pl.semaphore_signal(
            barrier, inc=1, device_id=(lax.rem(y + k, 4) * 8 + z, h), device_id_type=MESH
        )
    pl.semaphore_wait(barrier, 17)
    for copy in own:
        copy.wait()

    def remote(src, dst, send, recv, to):
        return pltpu.make_async_remote_copy(
            src, dst, send, recv, device_id=to, device_id_type=MESH
        )

    def chunk(p, dy, dz):
        b, _, first, rows, shard, left, width = PIECES[p]
        position = z_at(dz) if b == 1 else y_at(dy) * 8 + z_at(dz)
        row = pl.multiple_of(position * shard + first, 16)
        return bufs[b].at[pl.ds(row, rows), pl.ds(left, width)]

    def spread(p, dy, dz, only="zy"):
        ref = chunk(p, dy, dz)
        if p == MIX and dy == 0 and only == "zy":
            only = "z"
        for link, target in forwards(PIECES[p][1], dy, dz):
            if link[0] not in only:
                continue
            remote(ref, ref, ssem.at[p], rsem.at[PLACES[p][target]], (links[link], h)).start()

    def arrived(p, dy, dz):
        ref = chunk(p, dy, dz)
        remote(ref, ref, ssem.at[p], rsem.at[PLACES[p][dy, dz]], (links["z+"], h)).wait_recv()

    def ended(p):
        b, tree, _, rows, _, left, width = PIECES[p]
        last = ends(tree)
        ref = bufs[b].at[pl.ds(0, len(last) * rows), pl.ds(left, width)]
        remote(ref, ref, ssem.at[p], rsem.at[PLACES[p][last[0]]], (links["z+"], h)).wait_recv()

    def over_head(refs, send, recvs, four, seven):
        def push(owner, to, slot):
            remote(refs(owner), refs(owner), send, recvs(slot), (c, to)).start()

        def take(ref, slot):
            remote(ref, ref, send, recvs(slot), (c, sib)).wait_recv()

        def begin():
            push(h, xp, 0)
            push(h, xm, 1)
            push(h, sib, 3)

        def one():
            take(refs(xm), 0)
            push(xm, xp, 2)
            push(xm, sib, 3)
            take(refs(xp), 1)
            push(xp, sib, 3)

        def two():
            take(refs(xd), 2)
            push(xd, sib, 3)

        def three():
            take(four, 3)

        def drain():
            remote(seven, seven, send, recvs(0), (c, sib)).wait_send()

        return begin, one, two, three, drain

    enc_steps = over_head(
        lambda o: encb.at[o], es.at[0], lambda n: er.at[n], encb.at[pl.ds(0, 4)], encb.at[pl.ds(0, 7)]
    )
    ag_steps = [
        over_head(
            lambda o, g=g: nbuf.at[pl.ds(pl.multiple_of(o * 16, 16), 16), pl.ds(1536 * g, 1536)],
            gs.at[g],
            lambda n, g=g: gr.at[g, n],
            nbuf.at[pl.ds(0, 64), pl.ds(1536 * g, 1536)],
            nbuf.at[pl.ds(0, 112), pl.ds(1536 * g, 1536)],
        )
        for g in range(2)
    ]
    enc_steps[0]()

    def norm(v):
        return v * lax.rsqrt(jnp.mean(v * v, axis=-1, keepdims=True) + 1e-05) * gain[...]

    def hid_ref(dy, q):
        return hidb.at[y_at(dy), :, pl.ds(384 * q, 384)]

    def hid_send(dy, q, link, at):
        slot = {-1: 0, 1: 1, -2: 2}[at]
        return remote(hid_ref(dy, q), hid_ref(dy, q), hs.at[0], hr.at[slot, q], (links[link], h))

    def placed(i):
        cols = pl.ds(512 * i, 512)
        moved = dot(put[...], q_i[:, cols], ((0,), (0,)))
        qkv[:, cols] = jnp.where(
            hit[:, 0:1] > 0.5, moved, qkv[:, cols].astype(F32)
        ).astype(BF16)

    def to_z(k, src, dst, send, recv):
        zz = lax.rem(z + k, 8)
        return remote(src.at[zz], dst, send.at[0], recv.at[0], (y * 8 + zz, h))

    far_first = (4, 3, 5, 2, 6, 1, 7)
    mine_z = pl.ds(pl.multiple_of(z * 64, 64), 64)
    z_first = [to_z(k, st_s, st_r.at[z], sem_s, sem_r) for k in far_first]
    z_last = [to_z(k, pre_s, pre.at[mine_z], psem_s, psem_r) for k in far_first]
    y_sums = [
        remote(y_s, y_r.at[y], ysem_s.at[0], ysem_r.at[0], (lax.rem(y + k, 4) * 8 + z, h))
        for k in (2, 1, 3)
    ]

    def all_of(ref, send, recv):
        return remote(ref, ref, send.at[0], recv.at[0], (links["z+"], h))

    z_first_all = all_of(st_r.at[pl.ds(0, 7)], sem_s, sem_r)
    y_sums_all = all_of(y_r.at[pl.ds(0, 3)], ysem_s, ysem_r)
    z_last_all = all_of(st_s.at[pl.ds(0, 7)], psem_s, psem_r)

    for event in ORDER:
        kind = event[0]
        if kind == "own":
            spread(event[1], 0, 0)
        elif kind == "rx":
            arrived(*event[1:])
            spread(*event[1:])
        elif kind == "ends":
            ended(event[1])
        elif kind == "fan":
            for dz in (0, -1, 1, -2, 2, -3, 3, -4):
                spread(MIX, 0, dz, "y")
        elif kind == "norm":
            if event[1] == 0:
                load_x.wait()
            rows = pl.ds(64 * event[1], 64)
            xs[rows, :] = norm(xs[rows, :].astype(F32)).astype(BF16)
        elif kind == "stream":
            i, part_of = divmod(event[1], 4)
            if part_of == 0:
                load_w[i].wait()
                if i < 2:
                    load_w[i + 1].start()
            half, low = divmod(part_of, 2)
            rows = pl.ds(256 * low, 256)
            value = silu(dot(xs[rows, :], wq[i, :, pl.ds(256 * half, 256)], ((1,), (0,))))
            qkv[rows, pl.ds(512 * i + 256 * half, 256)] = value.astype(BF16)
        elif kind == "put":
            rank = live_slots(counts)[0:1, :]
            row = lax.broadcasted_iota(jnp.int32, (128, 512), 0)
            local = places[...] - c * 512
            where = jnp.sum(jnp.where(row == rank, local, 0).astype(F32), axis=1, keepdims=True)
            token = lax.broadcasted_iota(jnp.int32, (128, 512), 1)
            put[...] = jnp.where(token == where.astype(jnp.int32), 1.0, 0.0).astype(BF16)
            hit[...] = dot(put[...], jnp.ones((128, 128), BF16), ((0,), (0,)))
        elif kind == "hid":
            q = event[1]
            if q == 0:
                rank = live_slots(counts)
                row = lax.broadcasted_iota(jnp.int32, (128, 512), 0)
                pick = jnp.where(row == rank[0:1, :], 1.0, 0.0).astype(BF16)
                rows_i[...] = dot(pick, encb[...].reshape(512, 1024), ((1,), (0,))).astype(BF16)
            cols = pl.ds(384 * q, 384)
            u = dot(rows_i[...], buf_a[:, cols], ((1,), (0,)))
            hidb[y, :, cols] = (0.5 * u * (1.0 + lax.erf(u * 0.7071067811865476))).astype(BF16)
            hid_send(0, q, "y+", -1).start()
            hid_send(0, q, "y-", 1).start()
        elif kind == "hy":
            dy, q = event[1:]
            hid_send(dy, q, "y+", dy).wait_recv()
            if dy == -1 and q == 0:
                hid_send(-1, 0, "y+", -2).start()
            elif dy == 1 and q == 1:
                hid_send(1, 1, "y-", -2).start()
        elif kind == "part":
            yy = y_at(event[1])
            pbuf[yy] = dot(hidb[yy], buf_b[...], ((1,), (1,))).astype(BF16)
            for k in range(1, 8):
                to = lax.rem(h + k, 8)
                remote(
                    pbuf.at[yy, pl.ds(pl.multiple_of(to * 16, 16), 16)],
                    rbuf.at[yy, h], ps.at[0], pr.at[yy], (c, to),
                ).start()
        elif kind == "rs":
            yy = y_at(event[1])
            total = pbuf[yy, pl.ds(pl.multiple_of(h * 16, 16), 16), :].astype(F32)
            ref = rbuf.at[yy, pl.ds(0, 7)]
            remote(ref, ref, ps.at[0], pr.at[yy], (c, sib)).wait_recv()
            for k in range(1, 8):
                total = total + rbuf[yy, lax.rem(h + k, 8)].astype(F32)
            here = pl.ds(pl.multiple_of(y * 768, 768), 768)
            if event[1] == 0:
                ibuf[:, here] = total.astype(BF16)
            else:
                isum[yy] = total.astype(BF16)
                remote(
                    isum.at[yy], ibuf.at[:, here], ts.at[0], tr.at[0], (yy * 8 + z, h)
                ).start()
        elif kind == "yi":
            ref = ibuf.at[:, pl.ds(0, 2304)]
            remote(ref, ref, ts.at[0], tr.at[0], (links["y+"], h)).wait_recv()
            mine = pl.ds(pl.multiple_of(h * 16, 16), 16)
            nbuf[mine, :] = norm(ibuf[...].astype(F32)).astype(BF16)
            for g in range(2):
                ag_steps[g][0]()
        elif kind in ("ag1", "ag2", "ag3"):
            ag_steps[event[1]][int(kind[2])]()
        elif kind in ("enc1", "enc2", "enc3"):
            enc_steps[int(kind[3])]()
        elif kind == "image":
            i = event[1]
            value = silu(dot(nbuf[...], wq[i], ((1,), (0,))))
            q_i[:, pl.ds(512 * i, 512)] = value.astype(BF16)
            if i == 0:
                placed(0)
        elif kind == "state":
            placed(1)
            placed(2)
            for i in range(4):
                k_i = qkv[:, pl.ds(512 + 128 * i, 128)]
                v_i = qkv[:, pl.ds(1024 + 128 * i, 128)]
                state = dot(k_i, v_i, ((0,), (0,))).astype(BF16)
                st_s[2 * i] = state[0:64]
                st_s[2 * i + 1] = state[64:128]
            for copy in z_first:
                copy.start()
            st_r[z] = st_s[z]
        elif kind == "local":
            i = event[1]
            causal = lax.broadcasted_iota(jnp.int32, (512, 512), 0) >= lax.broadcasted_iota(
                jnp.int32, (512, 512), 1
            )
            q_h = qkv[:, pl.ds(128 * i, 128)]
            k_h = qkv[:, pl.ds(512 + 128 * i, 128)]
            v_h = qkv[:, pl.ds(1024 + 128 * i, 128)]
            sc = jnp.where(causal, dot(q_h, k_h, ((1,), (1,))), 0.0).astype(BF16)
            att[:, pl.ds(128 * i, 128)] = dot(sc, v_h, ((1,), (0,)))
        elif kind == "z1":
            z_first_all.wait_recv()
            total = st_r[0].astype(F32)
            for k in range(1, 8):
                total = total + st_r[k].astype(F32)
            y_s[...] = total.astype(BF16)
            for copy in y_sums:
                copy.start()
            y_r[y] = y_s[...]
        elif kind == "y1":
            y_sums_all.wait_recv()
            run = jnp.zeros((64, 128), F32)
            for k in range(4):
                run = run + jnp.where(k < y, y_r[k].astype(F32), 0.0)
            for k in range(8):
                pre_s[k] = run.astype(BF16)
                run = run + st_r[k].astype(F32)
            for copy in z_last:
                copy.start()
            pre[mine_z, :] = pre_s[z]
        elif kind == "z2":
            z_last_all.wait_recv()

    for i in range(4):
        cols = pl.ds(128 * i, 128)
        a = att[:, cols] + dot(qkv[:, cols], pre[cols, :], ((1,), (0,)))
        a = a * lax.rsqrt(jnp.mean(a * a, axis=-1, keepdims=True) + 1e-06)
        ho[:, cols] = (a * hg[:, cols]).astype(BF16)

    def chip(f):
        return lax.rem(x + s * f + 4, 4)

    def to_sib(f, m):
        rows = pl.ds(256 * m, 256)
        theirs = pl.multiple_of(chip(f) * 768 + 384 * (1 - core), 384)
        return pltpu.make_async_remote_copy(
            part.at[rows, pl.ds(theirs, 384)], sibb.at[chip(f), rows],
            bsem_s, bsem_r.at[chip(f), m], device_id=(c, sib), device_id_type=MESH,
        )

    def mixed(f, m):
        rows = pl.ds(256 * m, 256)
        cols = pl.ds(pl.multiple_of(chip(f) * 768, 768), 768)
        part[rows, cols] = dot(ho[rows, :], mix[cols, :], ((1,), (1,))).astype(BF16)
        to_sib(f, m).start()

    def on_x(n, m):
        rows = pl.ds(256 * m, 256)
        dst = chain.at[rows] if n == 0 else fin.at[n - 1, rows]
        return pltpu.make_async_remote_copy(
            pair.at[n, rows], dst, csem_s.at[0], csem_r.at[n, m],
            device_id=(c, xm if n == 2 else xp), device_id_type=MESH,
        )

    def paired(f, m):
        rows = pl.ds(256 * m, 256)
        to_sib(f, m).wait_recv()
        ours = pl.ds(pl.multiple_of(chip(f) * 768 + 384 * core, 384), 384)
        return part[rows, ours].astype(F32) + sibb[chip(f), rows].astype(F32)

    def send(f, m):
        rows = pl.ds(256 * m, 256)
        n = {2: 0, 1: 1, -1: 2}[f]
        value = paired(f, m)
        if n == 1:
            on_x(0, m).wait_recv()
            value = value + chain[rows, :].astype(F32)
        pair[n, rows] = value.astype(BF16)
        on_x(n, m).start()

    mixed(2, 0)
    mixed(2, 1)
    send(2, 0)
    mixed(-1, 0)
    send(2, 1)
    mixed(1, 0)
    mixed(-1, 1)
    send(-1, 0)
    mixed(1, 1)
    send(-1, 1)
    send(1, 0)
    mixed(0, 0)
    send(1, 1)
    mixed(0, 1)
    for m in range(2):
        rows = pl.ds(256 * m, 256)
        value = paired(0, m)
        on_x(2, m).wait_recv()
        value = value + fin[1, rows].astype(F32)
        on_x(1, m).wait_recv()
        out[rows, :] = (value + fin[0, rows].astype(F32)).astype(BF16)

    for copies in (z_first_all, y_sums_all, z_last_all):
        copies.wait_send()
    remote(sibb, sibb, bsem_s, bsem_r.at[0, 0], (c, sib)).wait_send()
    remote(buf_b, buf_b, csem_s.at[0], csem_r.at[0, 0], (c, xp)).wait_send()
    for p, (b, _, _, rows, _, left, width) in enumerate(PIECES):
        ref = bufs[b].at[pl.ds(0, CHUNKS[p] * rows), pl.ds(left, width)]
        remote(ref, ref, ssem.at[p], rsem.at[0], (links["z+"], h)).wait_send()
    ref = buf_b.at[pl.ds(0, 384)]
    remote(ref, ref, hs.at[0], hr.at[0, 0], (links["y+"], h)).wait_send()
    ref = buf_b.at[pl.ds(0, 448)]
    remote(ref, ref, ps.at[0], pr.at[0], (c, sib)).wait_send()
    ref = isum.at[pl.ds(0, 3)]
    remote(ref, ref, ts.at[0], tr.at[0], (links["y+"], h)).wait_send()
    enc_steps[4]()
    for g in range(2):
        ag_steps[g][4]()


def on_device(
    enc_rows, row_counts, row_places, stream, norm_gain, proj_in, proj_out, qkv_weight, head_gain, mix_weight
):
    vmem = pl.BlockSpec(memory_space=pltpu.VMEM)
    smem = pl.BlockSpec(memory_space=pltpu.SMEM)
    hbm = pl.BlockSpec(memory_space=pl.ANY)
    dma = pltpu.SemaphoreType.DMA

    def b16(*shape):
        return pltpu.VMEM(shape, BF16)

    def f32(*shape):
        return pltpu.VMEM(shape, F32)

    return pl.pallas_call(
        kernel,
        out_shape=jax.ShapeDtypeStruct((512, 384), BF16),
        in_specs=[smem, vmem, vmem, hbm, hbm, vmem, hbm, hbm, hbm, hbm],
        out_specs=vmem,
        scratch_shapes=[
            b16(1024, 768), b16(768, 768), b16(3072, 512), b16(3, 3072, 512), b16(512, 3072),
            b16(8, 64, 1024), b16(128, 1024), b16(4, 128, 768), b16(4, 128, 768), b16(4, 8, 16, 768),
            b16(4, 16, 768), b16(16, 3072), b16(128, 3072), b16(128, 1536), b16(128, 512),
            f32(512, 128),
            b16(512, 1536), b16(8, 64, 128), b16(8, 64, 128), b16(64, 128), b16(4, 64, 128),
            b16(8, 64, 128), b16(512, 128), f32(512, 512), b16(512, 512), b16(512, 3072),
            b16(4, 512, 384), b16(3, 512, 384), b16(512, 384), b16(2, 512, 384),
            dma((5,)), dma((3,)), dma((len(PIECES),)), dma((ARRIVALS,)), dma((1,)), dma((4,)),
            dma((1,)), dma((3, 2)), dma((1,)), dma((4,)), dma((1,)), dma((1,)),
            dma((2,)), dma((2, 4)),
            dma((1,)), dma((1,)), dma((1,)), dma((1,)), dma((1,)), dma((1,)),
            dma, dma((4, 2)), dma((1,)), dma((3, 2)),
        ],
        compiler_params=pltpu.CompilerParams(
            collective_id=0, has_side_effects=True, vmem_limit_bytes=VMEM_BYTES
        ),
        name="project_attend_mix",
    )(
        row_counts, row_places, head_gain.reshape(1, -1), enc_rows, stream,
        norm_gain.reshape(1, -1), proj_in, proj_out.T, mix_weight.T, qkv_weight.transpose(1, 0, 2),
    )


def solution(mesh):
    in_specs = (
        P(("ctx", "head"), None),
        P("ctx", None),
        P("ctx", None),
        P("ctx", None),
        P(),
        P("ctx", "head"),
        P("head", "ctx"),
        P(None, None, "head"),
        P("head"),
        P("head", "ctx"),
    )
    out_specs = P("ctx", "head")
    return jax.shard_map(
        on_device, mesh=mesh, in_specs=in_specs, out_specs=out_specs, check_vma=False
    )
```

```python
import heapq

import jax
import jax.numpy as jnp
from jax import lax
from jax.experimental import pallas as pl
from jax.experimental.pallas import tpu as pltpu
from jax.sharding import PartitionSpec as P

MESH = pl.DeviceIdType.MESH
BF16 = jnp.bfloat16
F32 = jnp.float32
VMEM_BYTES = 67043328 - 434176

PIECES = (
    (0, "A", 0, 32, 32, 0, 384),
    (0, "A", 0, 32, 32, 384, 384),
    (1, "z", 0, 32, 96, 0, 768),
    (1, "z", 32, 32, 96, 0, 768),
    (1, "z", 64, 32, 96, 0, 768),
    (2, "A", 0, 64, 96, 0, 512),
    (2, "b", 64, 32, 96, 0, 512),
)
CHUNKS = (31, 31, 7, 7, 7, 31, 31)
RELEASE = (0, 0, 4, 4, 4, 83, 83)
MIX = 5
SLACK = 1.5
EARLY, LATE = 0.5, 0.9


def forwards(tree, dy, dz):
    out = []
    along_z = []
    if -4 < dz <= 0:
        along_z.append(("z+", (dy, dz - 1)))
    if 0 <= dz < 3:
        along_z.append(("z-", (dy, dz + 1)))
    if tree == "z":
        return along_z
    if tree in "aA":
        if tree == "A":
            along_z = {
                -2: [("z+", (0, -3)), ("zz+", (0, -4))],
                0: [("z+", (0, -1)), ("z-", (0, 1)), ("zz+", (0, -2)), ("zz-", (0, 2))],
                2: [("z-", (0, 3))],
            }.get(dz, [])
        if dy == 0:
            out += along_z + [("y+", (-1, dz)), ("y-", (1, dz))]
        elif dy == -1 and dz % 2 == 0:
            out.append(("y+", (-2, dz)))
        elif dy == 1 and dz % 2 != 0:
            out.append(("y-", (-2, dz)))
    else:
        if dz == 0:
            if dy == 0:
                out += [("y+", (-1, 0)), ("y-", (1, 0))]
            elif dy == -1:
                out.append(("y+", (-2, 0)))
        out += along_z
    return out


def ends(tree):
    out = []
    for dy in ((0,) if tree == "z" else (-2, -1, 0, 1)):
        for dz in range(-4, 4):
            if (dy, dz) != (0, 0) and not forwards(tree, dy, dz):
                out.append((dy, dz))
    return out


def semaphores():
    places, total = [], 0
    for _, tree, *_ in PIECES:
        last = ends(tree)
        place = dict.fromkeys(last, total)
        total += 1
        for dy in ((0,) if tree == "z" else (-2, -1, 0, 1)):
            for dz in range(-4, 4):
                if (dy, dz) != (0, 0) and (dy, dz) not in place:
                    place[dy, dz] = total
                    total += 1
        places.append(place)
    return places, total


def plan():
    rate, hop = 46.5e3, 2.3
    free = dict.fromkeys(("z+", "z-", "y+", "y-", "x"), 0.0)
    now, count, order, heap = 0.0, 0, [], []
    released, left = set(), list(CHUNKS)
    tasks = [(("norm", i), 0.2) for i in range(8)] + [(("stream", i), 1.0) for i in range(12)]
    tasks.insert(16, (("put",), 0.4))
    near_y, near_z, fan_left, fanned, gathered, urgent = 6, 7, 7, False, False, False
    last = [ends(piece[1]) for piece in PIECES]
    open_ends = [len(e) for e in last]
    hids, waiting, ready, summed = 0, {0: 2, -1: 2, 1: 2, -2: 2}, [], 0
    for at, name in ((7.5, "enc1"), (11.0, "enc2"), (14.0, "enc3")):
        heapq.heappush(heap, (at, (name,)))

    def later(delay, *event):
        heapq.heappush(heap, (now + delay, event))

    def travel(link, size, *event):
        if link[:2] == "zz":
            link, size = link[1:], 2 * size
        free[link] = max(free[link], now) + size / rate
        first = 1.8 if now < 1.0 else 0.0
        slack = SLACK if event[0] == "rx" and event[1] >= MIX else 0.0
        heapq.heappush(heap, (free[link] + hop + first + slack, event))

    def size_of(p):
        return PIECES[p][3] * PIECES[p][6] * 2

    def issue(p, dy, dz):
        for link, target in forwards(PIECES[p][1], dy, dz):
            if p == MIX and dy == 0 and link[0] == "y" and not fanned:
                continue
            travel(link, size_of(p), "rx", p, *target)

    while True:
        for p in range(len(PIECES)):
            if p not in released and count >= RELEASE[p] and (p <= MIX or near_y == 0):
                released.add(p)
                order.append(("own", p))
                issue(p, 0, 0)
        if gathered and fan_left == 0 and not fanned:
            fanned = True
            order.append(("fan",))
            for dz in (0, -1, 1, -2, 2, -3, 3, -4):
                for link, target in forwards("a", 0, dz):
                    if link[0] == "y":
                        travel(link, size_of(MIX), "rx", MIX, *target)
        if heap and heap[0][0] <= now:
            event = heapq.heappop(heap)[1]
            kind = event[0]
            if kind == "rx" and event[2:] in last[event[1]]:
                p = event[1]
                count += 1
                left[p] -= 1
                open_ends[p] -= 1
                fan_left -= p == MIX and event[2] == 0
                near_z -= p == 0 and event[2] == 0
                if open_ends[p] == 0:
                    order.append(("ends", p))
                continue
            order.append(event)
            if kind == "rx":
                _, p, dy, dz = event
                count += 1
                left[p] -= 1
                fan_left -= p == MIX and dy == 0
                near_z -= p == 0 and dy == 0
                issue(p, dy, dz)
            elif kind == "hy":
                _, dy, q = event
                if dy == -1 and q == 0:
                    travel("y+", 98304, "hy", -2, 0)
                elif dy == 1 and q == 1:
                    travel("y-", 98304, "hy", -2, 1)
                waiting[dy] -= 1
                near_y -= 1
                if waiting[dy] == 0:
                    ready.append(dy)
            elif kind == "rs":
                now += 0.1
                summed += 1
                if summed == 4:
                    later(3.6, "yi")
            elif kind == "yi":
                now += 0.4
                gathered = True
                for g in range(2):
                    later(3.6 + g, "ag1", g)
                    later(6.2 + g, "ag2", g)
                    later(7.4 + g, "ag3", g)
            elif kind == "ag3":
                urgent = True
                if event[1] == 0:
                    tasks += [(("image", 1, 0), 0.4), (("image", 2, 0), 0.4)]
                else:
                    tasks += [(("image", 1, 1), 0.4), (("image", 2, 1), 0.4), (("state",), 1.0), (("image", 0, 0), 0.4), (("image", 0, 1), 0.4)]
            elif kind == "z1":
                now += 0.1
                later(3.6, "y1")
            elif kind == "y1":
                now += 0.4
                later(5.2, "z2")
            continue
        if hids < 2 and left[hids] == 0 and ("enc3",) in order:
            order.append(("hid", hids))
            now += 0.6 if hids == 0 else 0.4
            travel("y+", 98304, "hy", -1, hids)
            travel("y-", 98304, "hy", 1, hids)
            hids += 1
            if hids == 2:
                ready.append(0)
            continue
        if ready and sum(left[2:MIX]) == 0:
            dy = ready.pop(0)
            order.append(("part", dy))
            now += 0.65
            travel("x", 98304, "rs", dy)
            continue
        if tasks and (
            urgent or not heap or heap[0][0] >= now + (LATE if hids == 2 else EARLY) * tasks[0][1]
        ) and (near_z == 0 or tasks[0][0][0] == "norm"):
            task, time = tasks.pop(0)
            order.append(task)
            now += time
            if task == ("state",):
                later(5.0, "z1")
            elif task == ("image", 0, 1):
                tasks += [(("local", i), 0.55) for i in range(4)]
            continue
        if not heap:
            return order
        now = max(now, heap[0][0])


ORDER = plan()
PLACES, ARRIVALS = semaphores()


def dot(a, b, dims):
    return lax.dot_general(a, b, (dims, ((), ())), preferred_element_type=F32)


def silu(v):
    return v * jax.nn.sigmoid(v)


def live_slots(counts_ref):
    slot = lax.broadcasted_iota(jnp.int32, (8, 512), 1)
    rank = jnp.full((8, 512), -1, jnp.int32)
    before = jnp.int32(0)
    for h in range(8):
        count = counts_ref[0, h]
        within = slot - 64 * h
        mine = (within >= 0) & (within < 64) & (within < count)
        rank = jnp.where(mine, within + before, rank)
        before = before + count
    return rank


def place_of_me():
    c, h = lax.axis_index("ctx"), lax.axis_index("head")
    y, z, x, core = c // 8, c % 8, h // 2, h % 2
    return c, h, y, z, x, core, 1 - 2 * core


def kernel(
    counts, places, hg, enc, stream, gain, a_in, b_in, c_in, w_in,
    out,
    buf_a, buf_b, mix, wq, xs, encb, rows_i, hidb, pbuf, rbuf, isum, ibuf, nbuf, q_i, put, hit,
    qkv, st_s, st_r, y_s, y_r, pre_s, pre, att, ho, part, sibb, pair, chain, fin,
    lsem, wsem, ssem, rsem, es, er, hs, hr, ps, pr, ts, tr, gs, gr,
    sem_s, sem_r, ysem_s, ysem_r, psem_s, psem_r, bsem_s, bsem_r, csem_s, csem_r,
):
    c, h, y, z, x, core, s = place_of_me()
    bufs = (buf_a, buf_b, mix)
    own = []
    bases = (c * 32, z * 96, c * 96)
    for i, (src, buf, rows) in enumerate(((a_in, buf_a, 32), (b_in, buf_b, 96), (c_in, mix, 96))):
        own.append(
            pltpu.make_async_copy(src, buf.at[pl.ds(pl.multiple_of(bases[i], 32), rows)], lsem.at[i])
        )
    load_x = pltpu.make_async_copy(stream, xs, lsem.at[3])
    own.append(pltpu.make_async_copy(enc, encb.at[h], lsem.at[4]))
    load_w = [pltpu.make_async_copy(w_in.at[i], wq.at[i], wsem.at[i]) for i in range(3)]
    for copy in own:
        copy.start()
    load_x.start()
    load_w[0].start()

    def y_at(dy):
        return lax.rem(y + s * dy + 8, 4)

    def z_at(dz):
        return lax.rem(z + s * dz + 16, 8)

    links = {
        "z+": y * 8 + z_at(1), "z-": y * 8 + z_at(-1), "y+": y_at(1) * 8 + z, "y-": y_at(-1) * 8 + z,
        "zz+": y * 8 + z_at(2), "zz-": y * 8 + z_at(-2),
    }
    sib = 2 * x + 1 - core
    xp = 2 * lax.rem(x + s + 4, 4) + core
    xm = 2 * lax.rem(x - s + 4, 4) + core
    xd = 2 * lax.rem(x + 2, 4) + core

    barrier = pltpu.get_barrier_semaphore()
    for k in range(1, 8):
        pl.semaphore_signal(
            barrier, inc=1, device_id=(y * 8 + lax.rem(z + k, 8), h), device_id_type=MESH
        )
        pl.semaphore_signal(
            barrier, inc=1, device_id=(c, lax.rem(h + k, 8)), device_id_type=MESH
        )
    for k in range(1, 4):
        pl.semaphore_signal(
            barrier, inc=1, device_id=(lax.rem(y + k, 4) * 8 + z, h), device_id_type=MESH
        )
    pl.semaphore_wait(barrier, 17)
    for copy in own:
        copy.wait()

    def remote(src, dst, send, recv, to):
        return pltpu.make_async_remote_copy(
            src, dst, send, recv, device_id=to, device_id_type=MESH
        )

    def chunk(p, dy, dz):
        b, _, first, rows, shard, left, width = PIECES[p]
        position = z_at(dz) if b == 1 else y_at(dy) * 8 + z_at(dz)
        row = pl.multiple_of(position * shard + first, 16)
        return bufs[b].at[pl.ds(row, rows), pl.ds(left, width)]

    def spread(p, dy, dz, only="zy"):
        ref = chunk(p, dy, dz)
        if p == MIX and dy == 0 and only == "zy":
            only = "z"
        for link, target in forwards(PIECES[p][1], dy, dz):
            if link[0] not in only:
                continue
            remote(ref, ref, ssem.at[p], rsem.at[PLACES[p][target]], (links[link], h)).start()

    def arrived(p, dy, dz):
        ref = chunk(p, dy, dz)
        remote(ref, ref, ssem.at[p], rsem.at[PLACES[p][dy, dz]], (links["z+"], h)).wait_recv()

    def ended(p):
        b, tree, _, rows, _, left, width = PIECES[p]
        last = ends(tree)
        ref = bufs[b].at[pl.ds(0, len(last) * rows), pl.ds(left, width)]
        remote(ref, ref, ssem.at[p], rsem.at[PLACES[p][last[0]]], (links["z+"], h)).wait_recv()

    def over_head(refs, send, recvs, four, seven):
        def push(owner, to, slot):
            remote(refs(owner), refs(owner), send, recvs(slot), (c, to)).start()

        def take(ref, slot):
            remote(ref, ref, send, recvs(slot), (c, sib)).wait_recv()

        def begin():
            push(h, xp, 0)
            push(h, xm, 1)
            push(h, sib, 3)

        def one():
            take(refs(xm), 0)
            push(xm, xp, 2)
            push(xm, sib, 3)
            take(refs(xp), 1)
            push(xp, sib, 3)

        def two():
            take(refs(xd), 2)
            push(xd, sib, 3)

        def three():
            take(four, 3)

        def drain():
            remote(seven, seven, send, recvs(0), (c, sib)).wait_send()

        return begin, one, two, three, drain

    enc_steps = over_head(
        lambda o: encb.at[o], es.at[0], lambda n: er.at[n], encb.at[pl.ds(0, 4)], encb.at[pl.ds(0, 7)]
    )
    ag_steps = [
        over_head(
            lambda o, g=g: nbuf.at[pl.ds(pl.multiple_of(o * 16, 16), 16), pl.ds(1536 * g, 1536)],
            gs.at[g],
            lambda n, g=g: gr.at[g, n],
            nbuf.at[pl.ds(0, 64), pl.ds(1536 * g, 1536)],
            nbuf.at[pl.ds(0, 112), pl.ds(1536 * g, 1536)],
        )
        for g in range(2)
    ]
    enc_steps[0]()

    def norm(v):
        return v * lax.rsqrt(jnp.mean(v * v, axis=-1, keepdims=True) + 1e-05) * gain[...]

    def hid_ref(dy, q):
        return hidb.at[y_at(dy), :, pl.ds(384 * q, 384)]

    def hid_send(dy, q, link, at):
        slot = {-1: 0, 1: 1, -2: 2}[at]
        return remote(hid_ref(dy, q), hid_ref(dy, q), hs.at[0], hr.at[slot, q], (links[link], h))

    def placed(i):
        cols = pl.ds(512 * i, 512)
        moved = dot(put[...], q_i[:, cols], ((0,), (0,)))
        qkv[:, cols] = jnp.where(
            hit[:, 0:1] > 0.5, moved, qkv[:, cols].astype(F32)
        ).astype(BF16)

    def to_z(k, src, dst, send, recv):
        zz = lax.rem(z + k, 8)
        return remote(src.at[zz], dst, send.at[0], recv.at[0], (y * 8 + zz, h))

    far_first = (4, 3, 5, 2, 6, 1, 7)
    mine_z = pl.ds(pl.multiple_of(z * 64, 64), 64)
    z_first = [to_z(k, st_s, st_r.at[z], sem_s, sem_r) for k in far_first]
    z_last = [to_z(k, pre_s, pre.at[mine_z], psem_s, psem_r) for k in far_first]
    y_sums = [
        remote(y_s, y_r.at[y], ysem_s.at[0], ysem_r.at[0], (lax.rem(y + k, 4) * 8 + z, h))
        for k in (2, 1, 3)
    ]

    def all_of(ref, send, recv):
        return remote(ref, ref, send.at[0], recv.at[0], (links["z+"], h))

    z_first_all = all_of(st_r.at[pl.ds(0, 7)], sem_s, sem_r)
    y_sums_all = all_of(y_r.at[pl.ds(0, 3)], ysem_s, ysem_r)
    z_last_all = all_of(st_s.at[pl.ds(0, 7)], psem_s, psem_r)

    for event in ORDER:
        kind = event[0]
        if kind == "own":
            spread(event[1], 0, 0)
        elif kind == "rx":
            arrived(*event[1:])
            spread(*event[1:])
        elif kind == "ends":
            ended(event[1])
        elif kind == "fan":
            for dz in (0, -1, 1, -2, 2, -3, 3, -4):
                spread(MIX, 0, dz, "y")
        elif kind == "norm":
            if event[1] == 0:
                load_x.wait()
            rows = pl.ds(64 * event[1], 64)
            xs[rows, :] = norm(xs[rows, :].astype(F32)).astype(BF16)
        elif kind == "stream":
            i, part_of = divmod(event[1], 4)
            if part_of == 0:
                load_w[i].wait()
                if i < 2:
                    load_w[i + 1].start()
            half, low = divmod(part_of, 2)
            rows = pl.ds(256 * low, 256)
            value = silu(dot(xs[rows, :], wq[i, :, pl.ds(256 * half, 256)], ((1,), (0,))))
            qkv[rows, pl.ds(512 * i + 256 * half, 256)] = value.astype(BF16)
        elif kind == "put":
            rank = live_slots(counts)[0:1, :]
            row = lax.broadcasted_iota(jnp.int32, (128, 512), 0)
            local = places[...] - c * 512
            where = jnp.sum(jnp.where(row == rank, local, 0).astype(F32), axis=1, keepdims=True)
            token = lax.broadcasted_iota(jnp.int32, (128, 512), 1)
            put[...] = jnp.where(token == where.astype(jnp.int32), 1.0, 0.0).astype(BF16)
            hit[...] = dot(put[...], jnp.ones((128, 128), BF16), ((0,), (0,)))
        elif kind == "hid":
            q = event[1]
            if q == 0:
                rank = live_slots(counts)
                row = lax.broadcasted_iota(jnp.int32, (128, 512), 0)
                pick = jnp.where(row == rank[0:1, :], 1.0, 0.0).astype(BF16)
                rows_i[...] = dot(pick, encb[...].reshape(512, 1024), ((1,), (0,))).astype(BF16)
            cols = pl.ds(384 * q, 384)
            u = dot(rows_i[...], buf_a[:, cols], ((1,), (0,)))
            hidb[y, :, cols] = (0.5 * u * (1.0 + lax.erf(u * 0.7071067811865476))).astype(BF16)
            hid_send(0, q, "y+", -1).start()
            hid_send(0, q, "y-", 1).start()
        elif kind == "hy":
            dy, q = event[1:]
            hid_send(dy, q, "y+", dy).wait_recv()
            if dy == -1 and q == 0:
                hid_send(-1, 0, "y+", -2).start()
            elif dy == 1 and q == 1:
                hid_send(1, 1, "y-", -2).start()
        elif kind == "part":
            yy = y_at(event[1])
            pbuf[yy] = dot(hidb[yy], buf_b[...], ((1,), (1,))).astype(BF16)
            for k in range(1, 8):
                to = lax.rem(h + k, 8)
                remote(
                    pbuf.at[yy, pl.ds(pl.multiple_of(to * 16, 16), 16)],
                    rbuf.at[yy, h], ps.at[0], pr.at[yy], (c, to),
                ).start()
        elif kind == "rs":
            yy = y_at(event[1])
            total = pbuf[yy, pl.ds(pl.multiple_of(h * 16, 16), 16), :].astype(F32)
            ref = rbuf.at[yy, pl.ds(0, 7)]
            remote(ref, ref, ps.at[0], pr.at[yy], (c, sib)).wait_recv()
            for k in range(1, 8):
                total = total + rbuf[yy, lax.rem(h + k, 8)].astype(F32)
            here = pl.ds(pl.multiple_of(y * 768, 768), 768)
            if event[1] == 0:
                ibuf[:, here] = total.astype(BF16)
            else:
                isum[yy] = total.astype(BF16)
                remote(
                    isum.at[yy], ibuf.at[:, here], ts.at[0], tr.at[0], (yy * 8 + z, h)
                ).start()
        elif kind == "yi":
            ref = ibuf.at[:, pl.ds(0, 2304)]
            remote(ref, ref, ts.at[0], tr.at[0], (links["y+"], h)).wait_recv()
            mine = pl.ds(pl.multiple_of(h * 16, 16), 16)
            nbuf[mine, :] = norm(ibuf[...].astype(F32)).astype(BF16)
            for g in range(2):
                ag_steps[g][0]()
        elif kind in ("ag1", "ag2", "ag3"):
            ag_steps[event[1]][int(kind[2])]()
        elif kind in ("enc1", "enc2", "enc3"):
            enc_steps[int(kind[3])]()
        elif kind == "image":
            i, g = event[1:]
            half = pl.ds(1536 * g, 1536)
            value = dot(nbuf[:, half], wq[i, half, :], ((1,), (0,)))
            cols = pl.ds(512 * i, 512)
            if g == 0:
                att[pl.ds(128 * i, 128), :] = value
            else:
                q_i[:, cols] = silu(att[pl.ds(128 * i, 128), :] + value).astype(BF16)
            if i == 0 and g == 1:
                placed(0)
        elif kind == "state":
            placed(1)
            placed(2)
            for i in range(4):
                k_i = qkv[:, pl.ds(512 + 128 * i, 128)]
                v_i = qkv[:, pl.ds(1024 + 128 * i, 128)]
                state = dot(k_i, v_i, ((0,), (0,))).astype(BF16)
                st_s[2 * i] = state[0:64]
                st_s[2 * i + 1] = state[64:128]
            for copy in z_first:
                copy.start()
            st_r[z] = st_s[z]
        elif kind == "local":
            i = event[1]
            causal = lax.broadcasted_iota(jnp.int32, (512, 512), 0) >= lax.broadcasted_iota(
                jnp.int32, (512, 512), 1
            )
            q_h = qkv[:, pl.ds(128 * i, 128)]
            k_h = qkv[:, pl.ds(512 + 128 * i, 128)]
            v_h = qkv[:, pl.ds(1024 + 128 * i, 128)]
            sc = jnp.where(causal, dot(q_h, k_h, ((1,), (1,))), 0.0).astype(BF16)
            att[:, pl.ds(128 * i, 128)] = dot(sc, v_h, ((1,), (0,)))
        elif kind == "z1":
            z_first_all.wait_recv()
            total = st_r[0].astype(F32)
            for k in range(1, 8):
                total = total + st_r[k].astype(F32)
            y_s[...] = total.astype(BF16)
            for copy in y_sums:
                copy.start()
            y_r[y] = y_s[...]
        elif kind == "y1":
            y_sums_all.wait_recv()
            run = jnp.zeros((64, 128), F32)
            for k in range(4):
                run = run + jnp.where(k < y, y_r[k].astype(F32), 0.0)
            for k in range(8):
                pre_s[k] = run.astype(BF16)
                run = run + st_r[k].astype(F32)
            for copy in z_last:
                copy.start()
            pre[mine_z, :] = pre_s[z]
        elif kind == "z2":
            z_last_all.wait_recv()

    for i in range(4):
        cols = pl.ds(128 * i, 128)
        a = att[:, cols] + dot(qkv[:, cols], pre[cols, :], ((1,), (0,)))
        a = a * lax.rsqrt(jnp.mean(a * a, axis=-1, keepdims=True) + 1e-06)
        ho[:, cols] = (a * hg[:, cols]).astype(BF16)

    def chip(f):
        return lax.rem(x + s * f + 4, 4)

    def to_sib(f, m):
        rows = pl.ds(256 * m, 256)
        theirs = pl.multiple_of(chip(f) * 768 + 384 * (1 - core), 384)
        return pltpu.make_async_remote_copy(
            part.at[rows, pl.ds(theirs, 384)], sibb.at[chip(f), rows],
            bsem_s, bsem_r.at[chip(f), m], device_id=(c, sib), device_id_type=MESH,
        )

    def mixed(f, m):
        rows = pl.ds(256 * m, 256)
        cols = pl.ds(pl.multiple_of(chip(f) * 768, 768), 768)
        part[rows, cols] = dot(ho[rows, :], mix[cols, :], ((1,), (1,))).astype(BF16)
        to_sib(f, m).start()

    def on_x(n, m):
        rows = pl.ds(256 * m, 256)
        dst = chain.at[rows] if n == 0 else fin.at[n - 1, rows]
        return pltpu.make_async_remote_copy(
            pair.at[n, rows], dst, csem_s.at[0], csem_r.at[n, m],
            device_id=(c, xm if n == 2 else xp), device_id_type=MESH,
        )

    def paired(f, m):
        rows = pl.ds(256 * m, 256)
        to_sib(f, m).wait_recv()
        ours = pl.ds(pl.multiple_of(chip(f) * 768 + 384 * core, 384), 384)
        return part[rows, ours].astype(F32) + sibb[chip(f), rows].astype(F32)

    def send(f, m):
        rows = pl.ds(256 * m, 256)
        n = {2: 0, 1: 1, -1: 2}[f]
        value = paired(f, m)
        if n == 1:
            on_x(0, m).wait_recv()
            value = value + chain[rows, :].astype(F32)
        pair[n, rows] = value.astype(BF16)
        on_x(n, m).start()

    mixed(2, 0)
    mixed(2, 1)
    send(2, 0)
    mixed(-1, 0)
    send(2, 1)
    mixed(1, 0)
    mixed(-1, 1)
    send(-1, 0)
    mixed(1, 1)
    send(-1, 1)
    send(1, 0)
    mixed(0, 0)
    send(1, 1)
    mixed(0, 1)
    for m in range(2):
        rows = pl.ds(256 * m, 256)
        value = paired(0, m)
        on_x(2, m).wait_recv()
        value = value + fin[1, rows].astype(F32)
        on_x(1, m).wait_recv()
        out[rows, :] = (value + fin[0, rows].astype(F32)).astype(BF16)

    for copies in (z_first_all, y_sums_all, z_last_all):
        copies.wait_send()
    remote(sibb, sibb, bsem_s, bsem_r.at[0, 0], (c, sib)).wait_send()
    remote(buf_b, buf_b, csem_s.at[0], csem_r.at[0, 0], (c, xp)).wait_send()
    for p, (b, _, _, rows, _, left, width) in enumerate(PIECES):
        ref = bufs[b].at[pl.ds(0, CHUNKS[p] * rows), pl.ds(left, width)]
        remote(ref, ref, ssem.at[p], rsem.at[0], (links["z+"], h)).wait_send()
    ref = buf_b.at[pl.ds(0, 384)]
    remote(ref, ref, hs.at[0], hr.at[0, 0], (links["y+"], h)).wait_send()
    ref = buf_b.at[pl.ds(0, 448)]
    remote(ref, ref, ps.at[0], pr.at[0], (c, sib)).wait_send()
    ref = isum.at[pl.ds(0, 3)]
    remote(ref, ref, ts.at[0], tr.at[0], (links["y+"], h)).wait_send()
    enc_steps[4]()
    for g in range(2):
        ag_steps[g][4]()


def on_device(
    enc_rows, row_counts, row_places, stream, norm_gain, proj_in, proj_out, qkv_weight, head_gain, mix_weight
):
    vmem = pl.BlockSpec(memory_space=pltpu.VMEM)
    smem = pl.BlockSpec(memory_space=pltpu.SMEM)
    hbm = pl.BlockSpec(memory_space=pl.ANY)
    dma = pltpu.SemaphoreType.DMA

    def b16(*shape):
        return pltpu.VMEM(shape, BF16)

    def f32(*shape):
        return pltpu.VMEM(shape, F32)

    return pl.pallas_call(
        kernel,
        out_shape=pltpu.VMEM((512, 384), BF16),
        in_specs=[smem, vmem, vmem, hbm, hbm, vmem, hbm, hbm, hbm, hbm],
        out_specs=vmem,
        scratch_shapes=[
            b16(1024, 768), b16(768, 768), b16(3072, 512), b16(3, 3072, 512), b16(512, 3072),
            b16(8, 64, 1024), b16(128, 1024), b16(4, 128, 768), b16(4, 128, 768), b16(4, 8, 16, 768),
            b16(4, 16, 768), b16(16, 3072), b16(128, 3072), b16(128, 1536), b16(128, 512),
            f32(512, 128),
            b16(512, 1536), b16(8, 64, 128), b16(8, 64, 128), b16(64, 128), b16(4, 64, 128),
            b16(8, 64, 128), b16(512, 128), f32(512, 512), b16(512, 512), b16(512, 3072),
            b16(4, 512, 384), b16(3, 512, 384), b16(512, 384), b16(2, 512, 384),
            dma((5,)), dma((3,)), dma((len(PIECES),)), dma((ARRIVALS,)), dma((1,)), dma((4,)),
            dma((1,)), dma((3, 2)), dma((1,)), dma((4,)), dma((1,)), dma((1,)),
            dma((2,)), dma((2, 4)),
            dma((1,)), dma((1,)), dma((1,)), dma((1,)), dma((1,)), dma((1,)),
            dma, dma((4, 2)), dma((1,)), dma((3, 2)),
        ],
        compiler_params=pltpu.CompilerParams(
            collective_id=0, has_side_effects=True, vmem_limit_bytes=VMEM_BYTES
        ),
        name="project_attend_mix",
    )(
        row_counts, row_places, head_gain.reshape(1, -1), enc_rows, stream,
        norm_gain.reshape(1, -1), proj_in, proj_out.T, mix_weight.T, qkv_weight.transpose(1, 0, 2),
    )


def solution(mesh):
    in_specs = (
        P(("ctx", "head"), None),
        P("ctx", None),
        P("ctx", None),
        P("ctx", None),
        P(),
        P("ctx", "head"),
        P("head", "ctx"),
        P(None, None, "head"),
        P("head"),
        P("head", "ctx"),
    )
    out_specs = P("ctx", "head")
    return jax.shard_map(
        on_device, mesh=mesh, in_specs=in_specs, out_specs=out_specs, check_vma=False
    )
```

```python
import heapq

import jax
import jax.numpy as jnp
from jax import lax
from jax.experimental import pallas as pl
from jax.experimental.pallas import tpu as pltpu
from jax.sharding import PartitionSpec as P

MESH = pl.DeviceIdType.MESH
BF16 = jnp.bfloat16
F32 = jnp.float32
VMEM_BYTES = 67043328 - 434176

PIECES = (
    (0, "A", 0, 32, 32, 0, 384),
    (0, "A", 0, 32, 32, 384, 384),
    (1, "z", 0, 32, 96, 0, 768),
    (1, "z", 32, 32, 96, 0, 768),
    (1, "z", 64, 32, 96, 0, 768),
    (2, "A", 0, 64, 96, 0, 512),
    (2, "b", 64, 32, 96, 0, 512),
)
CHUNKS = (31, 31, 7, 7, 7, 31, 31)
RELEASE = (0, 0, 4, 4, 4, 83, 83)
MIX = 5
SLACK = 2.5
EARLY, LATE = 0.5, 0.9


def forwards(tree, dy, dz):
    out = []
    along_z = []
    if -4 < dz <= 0:
        along_z.append(("z+", (dy, dz - 1)))
    if 0 <= dz < 3:
        along_z.append(("z-", (dy, dz + 1)))
    if tree == "z":
        return along_z
    if tree in "aA":
        if tree == "A":
            along_z = {
                -2: [("z+", (0, -3)), ("zz+", (0, -4))],
                0: [("z+", (0, -1)), ("z-", (0, 1)), ("zz+", (0, -2)), ("zz-", (0, 2))],
                2: [("z-", (0, 3))],
            }.get(dz, [])
        if dy == 0:
            out += along_z + [("y+", (-1, dz)), ("y-", (1, dz))]
        elif dy == -1 and dz % 2 == 0:
            out.append(("y+", (-2, dz)))
        elif dy == 1 and dz % 2 != 0:
            out.append(("y-", (-2, dz)))
    else:
        if dz == 0:
            if dy == 0:
                out += [("y+", (-1, 0)), ("y-", (1, 0))]
            elif dy == -1:
                out.append(("y+", (-2, 0)))
        out += along_z
    return out


def ends(tree):
    out = []
    for dy in ((0,) if tree == "z" else (-2, -1, 0, 1)):
        for dz in range(-4, 4):
            if (dy, dz) != (0, 0) and not forwards(tree, dy, dz):
                out.append((dy, dz))
    return out


def semaphores():
    places, total = [], 0
    for _, tree, *_ in PIECES:
        last = ends(tree)
        place = dict.fromkeys(last, total)
        total += 1
        for dy in ((0,) if tree == "z" else (-2, -1, 0, 1)):
            for dz in range(-4, 4):
                if (dy, dz) != (0, 0) and (dy, dz) not in place:
                    place[dy, dz] = total
                    total += 1
        places.append(place)
    return places, total


def plan():
    rate, hop = 46.5e3, 2.3
    free = dict.fromkeys(("z+", "z-", "y+", "y-", "x"), 0.0)
    now, count, order, heap = 0.0, 0, [], []
    released, left = set(), list(CHUNKS)
    tasks = [(("norm", i), 0.2) for i in range(8)] + [(("stream", i), 1.0) for i in range(12)]
    tasks.insert(16, (("put",), 0.4))
    tasks.append((("base",), 0.8))
    near_y, near_z, fan_left, fanned, gathered, urgent = 6, 7, 7, False, False, False
    last = [ends(piece[1]) for piece in PIECES]
    open_ends = [len(e) for e in last]
    hids, waiting, ready, summed = 0, {0: 2, -1: 2, 1: 2, -2: 2}, [], 0
    for at, name in ((7.5, "enc1"), (11.0, "enc2"), (14.0, "enc3")):
        heapq.heappush(heap, (at, (name,)))

    def later(delay, *event):
        heapq.heappush(heap, (now + delay, event))

    def travel(link, size, *event):
        if link[:2] == "zz":
            link, size = link[1:], 2 * size
        free[link] = max(free[link], now) + size / rate
        first = 1.8 if now < 1.0 else 0.0
        slack = SLACK if event[0] == "rx" and event[1] >= MIX else 0.0
        heapq.heappush(heap, (free[link] + hop + first + slack, event))

    def size_of(p):
        return PIECES[p][3] * PIECES[p][6] * 2

    def issue(p, dy, dz):
        for link, target in forwards(PIECES[p][1], dy, dz):
            if p == MIX and dy == 0 and link[0] == "y" and not fanned:
                continue
            travel(link, size_of(p), "rx", p, *target)

    while True:
        for p in range(len(PIECES)):
            if p not in released and count >= RELEASE[p] and (p <= MIX or near_y == 0):
                released.add(p)
                order.append(("own", p))
                issue(p, 0, 0)
        if gathered and fan_left == 0 and not fanned:
            fanned = True
            order.append(("fan",))
            for dz in (0, -1, 1, -2, 2, -3, 3, -4):
                for link, target in forwards("a", 0, dz):
                    if link[0] == "y":
                        travel(link, size_of(MIX), "rx", MIX, *target)
        if heap and heap[0][0] <= now:
            event = heapq.heappop(heap)[1]
            kind = event[0]
            if kind == "rx" and event[2:] in last[event[1]]:
                p = event[1]
                count += 1
                left[p] -= 1
                open_ends[p] -= 1
                fan_left -= p == MIX and event[2] == 0
                near_z -= p == 0 and event[2] == 0
                if open_ends[p] == 0:
                    order.append(("ends", p))
                continue
            order.append(event)
            if kind == "rx":
                _, p, dy, dz = event
                count += 1
                left[p] -= 1
                fan_left -= p == MIX and dy == 0
                near_z -= p == 0 and dy == 0
                issue(p, dy, dz)
            elif kind == "hy":
                _, dy, q = event
                if dy == -1 and q == 0:
                    travel("y+", 98304, "hy", -2, 0)
                elif dy == 1 and q == 1:
                    travel("y-", 98304, "hy", -2, 1)
                waiting[dy] -= 1
                near_y -= 1
                if waiting[dy] == 0:
                    ready.append(dy)
            elif kind == "rs":
                now += 0.1
                summed += 1
                if summed == 4:
                    later(3.6, "yi")
            elif kind == "yi":
                now += 0.4
                gathered = True
                for g in range(2):
                    later(3.6 + g, "ag1", g)
                    later(6.2 + g, "ag2", g)
                    later(7.4 + g, "ag3", g)
            elif kind == "ag3":
                urgent = True
                if event[1] == 0:
                    tasks += [(("image", 1, 0), 0.4), (("image", 2, 0), 0.4)]
                else:
                    tasks += [(("image", 1, 1), 0.4), (("image", 2, 1), 0.4), (("state",), 1.0), (("image", 0, 0), 0.4), (("image", 0, 1), 0.4)]
            elif kind == "z1":
                now += 0.1
                later(3.6, "y1")
            elif kind == "y1":
                now += 0.4
                later(5.2, "z2")
            continue
        if hids < 2 and left[hids] == 0 and ("enc3",) in order:
            order.append(("hid", hids))
            now += 0.6 if hids == 0 else 0.4
            travel("y+", 98304, "hy", -1, hids)
            travel("y-", 98304, "hy", 1, hids)
            hids += 1
            if hids == 2:
                ready.append(0)
            continue
        if ready and sum(left[2:MIX]) == 0:
            dy = ready.pop(0)
            order.append(("part", dy))
            now += 0.65
            travel("x", 98304, "rs", dy)
            continue
        if tasks and (
            urgent or not heap or heap[0][0] >= now + (LATE if hids == 2 else EARLY) * tasks[0][1]
        ) and (near_z == 0 or tasks[0][0][0] == "norm"):
            task, time = tasks.pop(0)
            order.append(task)
            now += time
            if task == ("state",):
                later(5.0, "z1")
            elif task == ("image", 0, 1):
                tasks += [(("local", i), 0.55) for i in range(4)]
            continue
        if not heap:
            return order
        now = max(now, heap[0][0])


ORDER = plan()
PLACES, ARRIVALS = semaphores()


def dot(a, b, dims):
    return lax.dot_general(a, b, (dims, ((), ())), preferred_element_type=F32)


def silu(v):
    return v * jax.nn.sigmoid(v)


def live_slots(counts_ref):
    slot = lax.broadcasted_iota(jnp.int32, (8, 512), 1)
    rank = jnp.full((8, 512), -1, jnp.int32)
    before = jnp.int32(0)
    for h in range(8):
        count = counts_ref[0, h]
        within = slot - 64 * h
        mine = (within >= 0) & (within < 64) & (within < count)
        rank = jnp.where(mine, within + before, rank)
        before = before + count
    return rank


def place_of_me():
    c, h = lax.axis_index("ctx"), lax.axis_index("head")
    y, z, x, core = c // 8, c % 8, h // 2, h % 2
    return c, h, y, z, x, core, 1 - 2 * core


def kernel(
    counts, places, hg, enc, stream, gain, a_in, b_in, c_in, w_in,
    out,
    buf_a, buf_b, mix, wq, xs, encb, rows_i, hidb, pbuf, rbuf, isum, ibuf, nbuf, q_i, put, hit,
    qkv, st0, st_s, st_r, y_s, y_r, pre_s, pre, att, ho, part, sibb, pair, chain, fin,
    lsem, wsem, ssem, rsem, es, er, hs, hr, ps, pr, ts, tr, gs, gr,
    sem_s, sem_r, ysem_s, ysem_r, psem_s, psem_r, bsem_s, bsem_r, csem_s, csem_r,
):
    c, h, y, z, x, core, s = place_of_me()
    bufs = (buf_a, buf_b, mix)
    own = []
    bases = (c * 32, z * 96, c * 96)
    for i, (src, buf, rows) in enumerate(((a_in, buf_a, 32), (b_in, buf_b, 96), (c_in, mix, 96))):
        own.append(
            pltpu.make_async_copy(src, buf.at[pl.ds(pl.multiple_of(bases[i], 32), rows)], lsem.at[i])
        )
    load_x = pltpu.make_async_copy(stream, xs, lsem.at[3])
    own.append(pltpu.make_async_copy(enc, encb.at[h], lsem.at[4]))
    load_w = [pltpu.make_async_copy(w_in.at[i], wq.at[i], wsem.at[i]) for i in range(3)]
    for copy in own:
        copy.start()
    load_x.start()
    load_w[0].start()

    def y_at(dy):
        return lax.rem(y + s * dy + 8, 4)

    def z_at(dz):
        return lax.rem(z + s * dz + 16, 8)

    links = {
        "z+": y * 8 + z_at(1), "z-": y * 8 + z_at(-1), "y+": y_at(1) * 8 + z, "y-": y_at(-1) * 8 + z,
        "zz+": y * 8 + z_at(2), "zz-": y * 8 + z_at(-2),
    }
    sib = 2 * x + 1 - core
    xp = 2 * lax.rem(x + s + 4, 4) + core
    xm = 2 * lax.rem(x - s + 4, 4) + core
    xd = 2 * lax.rem(x + 2, 4) + core

    barrier = pltpu.get_barrier_semaphore()
    for k in range(1, 8):
        pl.semaphore_signal(
            barrier, inc=1, device_id=(y * 8 + lax.rem(z + k, 8), h), device_id_type=MESH
        )
        pl.semaphore_signal(
            barrier, inc=1, device_id=(c, lax.rem(h + k, 8)), device_id_type=MESH
        )
    for k in range(1, 4):
        pl.semaphore_signal(
            barrier, inc=1, device_id=(lax.rem(y + k, 4) * 8 + z, h), device_id_type=MESH
        )
    pl.semaphore_wait(barrier, 17)
    for copy in own:
        copy.wait()

    def remote(src, dst, send, recv, to):
        return pltpu.make_async_remote_copy(
            src, dst, send, recv, device_id=to, device_id_type=MESH
        )

    def chunk(p, dy, dz):
        b, _, first, rows, shard, left, width = PIECES[p]
        position = z_at(dz) if b == 1 else y_at(dy) * 8 + z_at(dz)
        row = pl.multiple_of(position * shard + first, 16)
        return bufs[b].at[pl.ds(row, rows), pl.ds(left, width)]

    def spread(p, dy, dz, only="zy"):
        ref = chunk(p, dy, dz)
        if p == MIX and dy == 0 and only == "zy":
            only = "z"
        for link, target in forwards(PIECES[p][1], dy, dz):
            if link[0] not in only:
                continue
            remote(ref, ref, ssem.at[p], rsem.at[PLACES[p][target]], (links[link], h)).start()

    def arrived(p, dy, dz):
        ref = chunk(p, dy, dz)
        remote(ref, ref, ssem.at[p], rsem.at[PLACES[p][dy, dz]], (links["z+"], h)).wait_recv()

    def ended(p):
        b, tree, _, rows, _, left, width = PIECES[p]
        last = ends(tree)
        ref = bufs[b].at[pl.ds(0, len(last) * rows), pl.ds(left, width)]
        remote(ref, ref, ssem.at[p], rsem.at[PLACES[p][last[0]]], (links["z+"], h)).wait_recv()

    def over_head(refs, send, recvs, four, seven):
        def push(owner, to, slot):
            remote(refs(owner), refs(owner), send, recvs(slot), (c, to)).start()

        def take(ref, slot):
            remote(ref, ref, send, recvs(slot), (c, sib)).wait_recv()

        def begin():
            push(h, xp, 0)
            push(h, xm, 1)
            push(h, sib, 3)

        def one():
            take(refs(xm), 0)
            push(xm, xp, 2)
            push(xm, sib, 3)
            take(refs(xp), 1)
            push(xp, sib, 3)

        def two():
            take(refs(xd), 2)
            push(xd, sib, 3)

        def three():
            take(four, 3)

        def drain():
            remote(seven, seven, send, recvs(0), (c, sib)).wait_send()

        return begin, one, two, three, drain

    enc_steps = over_head(
        lambda o: encb.at[o], es.at[0], lambda n: er.at[n], encb.at[pl.ds(0, 4)], encb.at[pl.ds(0, 7)]
    )
    ag_steps = [
        over_head(
            lambda o, g=g: nbuf.at[pl.ds(pl.multiple_of(o * 16, 16), 16), pl.ds(1536 * g, 1536)],
            gs.at[g],
            lambda n, g=g: gr.at[g, n],
            nbuf.at[pl.ds(0, 64), pl.ds(1536 * g, 1536)],
            nbuf.at[pl.ds(0, 112), pl.ds(1536 * g, 1536)],
        )
        for g in range(2)
    ]
    enc_steps[0]()

    def norm(v):
        return v * lax.rsqrt(jnp.mean(v * v, axis=-1, keepdims=True) + 1e-05) * gain[...]

    def hid_ref(dy, q):
        return hidb.at[y_at(dy), :, pl.ds(384 * q, 384)]

    def hid_send(dy, q, link, at):
        slot = {-1: 0, 1: 1, -2: 2}[at]
        return remote(hid_ref(dy, q), hid_ref(dy, q), hs.at[0], hr.at[slot, q], (links[link], h))

    def placed(i):
        cols = pl.ds(512 * i, 512)
        moved = dot(put[...], q_i[:, cols], ((0,), (0,)))
        qkv[:, cols] = jnp.where(
            hit[:, 0:1] > 0.5, moved, qkv[:, cols].astype(F32)
        ).astype(BF16)

    def to_z(k, src, dst, send, recv):
        zz = lax.rem(z + k, 8)
        return remote(src.at[zz], dst, send.at[0], recv.at[0], (y * 8 + zz, h))

    far_first = (4, 3, 5, 2, 6, 1, 7)
    mine_z = pl.ds(pl.multiple_of(z * 64, 64), 64)
    z_first = [to_z(k, st_s, st_r.at[z], sem_s, sem_r) for k in far_first]
    z_last = [to_z(k, pre_s, pre.at[mine_z], psem_s, psem_r) for k in far_first]
    y_sums = [
        remote(y_s, y_r.at[y], ysem_s.at[0], ysem_r.at[0], (lax.rem(y + k, 4) * 8 + z, h))
        for k in (2, 1, 3)
    ]

    def all_of(ref, send, recv):
        return remote(ref, ref, send.at[0], recv.at[0], (links["z+"], h))

    z_first_all = all_of(st_r.at[pl.ds(0, 7)], sem_s, sem_r)
    y_sums_all = all_of(y_r.at[pl.ds(0, 3)], ysem_s, ysem_r)
    z_last_all = all_of(st_s.at[pl.ds(0, 7)], psem_s, psem_r)

    for event in ORDER:
        kind = event[0]
        if kind == "own":
            spread(event[1], 0, 0)
        elif kind == "rx":
            arrived(*event[1:])
            spread(*event[1:])
        elif kind == "ends":
            ended(event[1])
        elif kind == "fan":
            for dz in (0, -1, 1, -2, 2, -3, 3, -4):
                spread(MIX, 0, dz, "y")
        elif kind == "norm":
            if event[1] == 0:
                load_x.wait()
            rows = pl.ds(64 * event[1], 64)
            xs[rows, :] = norm(xs[rows, :].astype(F32)).astype(BF16)
        elif kind == "stream":
            i, part_of = divmod(event[1], 4)
            if part_of == 0:
                load_w[i].wait()
                if i < 2:
                    load_w[i + 1].start()
            half, low = divmod(part_of, 2)
            rows = pl.ds(256 * low, 256)
            value = silu(dot(xs[rows, :], wq[i, :, pl.ds(256 * half, 256)], ((1,), (0,))))
            qkv[rows, pl.ds(512 * i + 256 * half, 256)] = value.astype(BF16)
        elif kind == "put":
            rank = live_slots(counts)[0:1, :]
            row = lax.broadcasted_iota(jnp.int32, (128, 512), 0)
            local = places[...] - c * 512
            where = jnp.sum(jnp.where(row == rank, local, 0).astype(F32), axis=1, keepdims=True)
            token = lax.broadcasted_iota(jnp.int32, (128, 512), 1)
            put[...] = jnp.where(token == where.astype(jnp.int32), 1.0, 0.0).astype(BF16)
            hit[...] = dot(put[...], jnp.ones((128, 128), BF16), ((0,), (0,)))
        elif kind == "hid":
            q = event[1]
            if q == 0:
                rank = live_slots(counts)
                row = lax.broadcasted_iota(jnp.int32, (128, 512), 0)
                pick = jnp.where(row == rank[0:1, :], 1.0, 0.0).astype(BF16)
                rows_i[...] = dot(pick, encb[...].reshape(512, 1024), ((1,), (0,))).astype(BF16)
            cols = pl.ds(384 * q, 384)
            u = dot(rows_i[...], buf_a[:, cols], ((1,), (0,)))
            hidb[y, :, cols] = (0.5 * u * (1.0 + lax.erf(u * 0.7071067811865476))).astype(BF16)
            hid_send(0, q, "y+", -1).start()
            hid_send(0, q, "y-", 1).start()
        elif kind == "hy":
            dy, q = event[1:]
            hid_send(dy, q, "y+", dy).wait_recv()
            if dy == -1 and q == 0:
                hid_send(-1, 0, "y+", -2).start()
            elif dy == 1 and q == 1:
                hid_send(1, 1, "y-", -2).start()
        elif kind == "part":
            yy = y_at(event[1])
            pbuf[yy] = dot(hidb[yy], buf_b[...], ((1,), (1,))).astype(BF16)
            for k in range(1, 8):
                to = lax.rem(h + k, 8)
                remote(
                    pbuf.at[yy, pl.ds(pl.multiple_of(to * 16, 16), 16)],
                    rbuf.at[yy, h], ps.at[0], pr.at[yy], (c, to),
                ).start()
        elif kind == "rs":
            yy = y_at(event[1])
            total = pbuf[yy, pl.ds(pl.multiple_of(h * 16, 16), 16), :].astype(F32)
            ref = rbuf.at[yy, pl.ds(0, 7)]
            remote(ref, ref, ps.at[0], pr.at[yy], (c, sib)).wait_recv()
            for k in range(1, 8):
                total = total + rbuf[yy, lax.rem(h + k, 8)].astype(F32)
            here = pl.ds(pl.multiple_of(y * 768, 768), 768)
            if event[1] == 0:
                ibuf[:, here] = total.astype(BF16)
            else:
                isum[yy] = total.astype(BF16)
                remote(
                    isum.at[yy], ibuf.at[:, here], ts.at[0], tr.at[0], (yy * 8 + z, h)
                ).start()
        elif kind == "yi":
            ref = ibuf.at[:, pl.ds(0, 2304)]
            remote(ref, ref, ts.at[0], tr.at[0], (links["y+"], h)).wait_recv()
            mine = pl.ds(pl.multiple_of(h * 16, 16), 16)
            nbuf[mine, :] = norm(ibuf[...].astype(F32)).astype(BF16)
            for g in range(2):
                ag_steps[g][0]()
        elif kind in ("ag1", "ag2", "ag3"):
            ag_steps[event[1]][int(kind[2])]()
        elif kind in ("enc1", "enc2", "enc3"):
            enc_steps[int(kind[3])]()
        elif kind == "image":
            i, g = event[1:]
            half = pl.ds(1536 * g, 1536)
            value = dot(nbuf[:, half], wq[i, half, :], ((1,), (0,)))
            cols = pl.ds(512 * i, 512)
            if g == 0:
                att[pl.ds(128 * i, 128), :] = value
            else:
                q_i[:, cols] = silu(att[pl.ds(128 * i, 128), :] + value).astype(BF16)
            if i == 0 and g == 1:
                placed(0)
        elif kind == "base":
            for i in range(4):
                k_i = qkv[:, pl.ds(512 + 128 * i, 128)].astype(F32)
                k_i = jnp.where(hit[:, 0:1] > 0.5, 0.0, k_i).astype(BF16)
                v_i = qkv[:, pl.ds(1024 + 128 * i, 128)]
                st0[pl.ds(128 * i, 128), :] = dot(k_i, v_i, ((0,), (0,)))
        elif kind == "state":
            for i in range(4):
                k_i = q_i[:, pl.ds(512 + 128 * i, 128)]
                v_i = q_i[:, pl.ds(1024 + 128 * i, 128)]
                state = st0[pl.ds(128 * i, 128), :] + dot(k_i, v_i, ((0,), (0,)))
                state = state.astype(BF16)
                st_s[2 * i] = state[0:64]
                st_s[2 * i + 1] = state[64:128]
            for copy in z_first:
                copy.start()
            st_r[z] = st_s[z]
            placed(1)
            placed(2)
        elif kind == "local":
            i = event[1]
            causal = lax.broadcasted_iota(jnp.int32, (512, 512), 0) >= lax.broadcasted_iota(
                jnp.int32, (512, 512), 1
            )
            q_h = qkv[:, pl.ds(128 * i, 128)]
            k_h = qkv[:, pl.ds(512 + 128 * i, 128)]
            v_h = qkv[:, pl.ds(1024 + 128 * i, 128)]
            sc = jnp.where(causal, dot(q_h, k_h, ((1,), (1,))), 0.0).astype(BF16)
            att[:, pl.ds(128 * i, 128)] = dot(sc, v_h, ((1,), (0,)))
        elif kind == "z1":
            z_first_all.wait_recv()
            total = st_r[0].astype(F32)
            for k in range(1, 8):
                total = total + st_r[k].astype(F32)
            y_s[...] = total.astype(BF16)
            for copy in y_sums:
                copy.start()
            y_r[y] = y_s[...]
        elif kind == "y1":
            y_sums_all.wait_recv()
            run = jnp.zeros((64, 128), F32)
            for k in range(4):
                run = run + jnp.where(k < y, y_r[k].astype(F32), 0.0)
            for k in range(8):
                pre_s[k] = run.astype(BF16)
                run = run + st_r[k].astype(F32)
            for copy in z_last:
                copy.start()
            pre[mine_z, :] = pre_s[z]
        elif kind == "z2":
            z_last_all.wait_recv()

    def finish(m):
        rows = pl.ds(256 * m, 256)
        for i in range(4):
            cols = pl.ds(128 * i, 128)
            a = att[rows, cols] + dot(qkv[rows, cols], pre[cols, :], ((1,), (0,)))
            a = a * lax.rsqrt(jnp.mean(a * a, axis=-1, keepdims=True) + 1e-06)
            ho[rows, cols] = (a * hg[:, cols]).astype(BF16)

    def chip(f):
        return lax.rem(x + s * f + 4, 4)

    def to_sib(f, m):
        rows = pl.ds(256 * m, 256)
        theirs = pl.multiple_of(chip(f) * 768 + 384 * (1 - core), 384)
        return pltpu.make_async_remote_copy(
            part.at[rows, pl.ds(theirs, 384)], sibb.at[chip(f), rows],
            bsem_s, bsem_r.at[chip(f), m], device_id=(c, sib), device_id_type=MESH,
        )

    def mixed(f, m):
        rows = pl.ds(256 * m, 256)
        cols = pl.ds(pl.multiple_of(chip(f) * 768, 768), 768)
        part[rows, cols] = dot(ho[rows, :], mix[cols, :], ((1,), (1,))).astype(BF16)
        to_sib(f, m).start()

    def on_x(n, m):
        rows = pl.ds(256 * m, 256)
        dst = chain.at[rows] if n == 0 else fin.at[n - 1, rows]
        return pltpu.make_async_remote_copy(
            pair.at[n, rows], dst, csem_s.at[0], csem_r.at[n, m],
            device_id=(c, xm if n == 2 else xp), device_id_type=MESH,
        )

    def paired(f, m):
        rows = pl.ds(256 * m, 256)
        to_sib(f, m).wait_recv()
        ours = pl.ds(pl.multiple_of(chip(f) * 768 + 384 * core, 384), 384)
        return part[rows, ours].astype(F32) + sibb[chip(f), rows].astype(F32)

    def send(f, m):
        rows = pl.ds(256 * m, 256)
        n = {2: 0, 1: 1, -1: 2}[f]
        value = paired(f, m)
        if n == 1:
            on_x(0, m).wait_recv()
            value = value + chain[rows, :].astype(F32)
        pair[n, rows] = value.astype(BF16)
        on_x(n, m).start()

    finish(0)
    mixed(2, 0)
    finish(1)
    mixed(2, 1)
    send(2, 0)
    mixed(-1, 0)
    send(2, 1)
    mixed(1, 0)
    mixed(-1, 1)
    send(-1, 0)
    mixed(1, 1)
    send(-1, 1)
    send(1, 0)
    mixed(0, 0)
    send(1, 1)
    mixed(0, 1)
    for m in range(2):
        rows = pl.ds(256 * m, 256)
        value = paired(0, m)
        on_x(2, m).wait_recv()
        value = value + fin[1, rows].astype(F32)
        on_x(1, m).wait_recv()
        out[rows, :] = (value + fin[0, rows].astype(F32)).astype(BF16)

    for copies in (z_first_all, y_sums_all, z_last_all):
        copies.wait_send()
    remote(sibb, sibb, bsem_s, bsem_r.at[0, 0], (c, sib)).wait_send()
    remote(buf_b, buf_b, csem_s.at[0], csem_r.at[0, 0], (c, xp)).wait_send()
    for p, (b, _, _, rows, _, left, width) in enumerate(PIECES):
        ref = bufs[b].at[pl.ds(0, CHUNKS[p] * rows), pl.ds(left, width)]
        remote(ref, ref, ssem.at[p], rsem.at[0], (links["z+"], h)).wait_send()
    ref = buf_b.at[pl.ds(0, 384)]
    remote(ref, ref, hs.at[0], hr.at[0, 0], (links["y+"], h)).wait_send()
    ref = buf_b.at[pl.ds(0, 448)]
    remote(ref, ref, ps.at[0], pr.at[0], (c, sib)).wait_send()
    ref = isum.at[pl.ds(0, 3)]
    remote(ref, ref, ts.at[0], tr.at[0], (links["y+"], h)).wait_send()
    enc_steps[4]()
    for g in range(2):
        ag_steps[g][4]()


def on_device(
    enc_rows, row_counts, row_places, stream, norm_gain, proj_in, proj_out, qkv_weight, head_gain, mix_weight
):
    vmem = pl.BlockSpec(memory_space=pltpu.VMEM)
    smem = pl.BlockSpec(memory_space=pltpu.SMEM)
    hbm = pl.BlockSpec(memory_space=pl.ANY)
    dma = pltpu.SemaphoreType.DMA

    def b16(*shape):
        return pltpu.VMEM(shape, BF16)

    def f32(*shape):
        return pltpu.VMEM(shape, F32)

    return pl.pallas_call(
        kernel,
        out_shape=pltpu.VMEM((512, 384), BF16),
        in_specs=[smem, vmem, vmem, hbm, hbm, vmem, hbm, hbm, hbm, hbm],
        out_specs=vmem,
        scratch_shapes=[
            b16(1024, 768), b16(768, 768), b16(3072, 512), b16(3, 3072, 512), b16(512, 3072),
            b16(8, 64, 1024), b16(128, 1024), b16(4, 128, 768), b16(4, 128, 768), b16(4, 8, 16, 768),
            b16(4, 16, 768), b16(16, 3072), b16(128, 3072), b16(128, 1536), b16(128, 512),
            f32(512, 128),
            b16(512, 1536), f32(512, 128), b16(8, 64, 128), b16(8, 64, 128), b16(64, 128), b16(4, 64, 128),
            b16(8, 64, 128), b16(512, 128), f32(512, 512), b16(512, 512), b16(512, 3072),
            b16(4, 512, 384), b16(3, 512, 384), b16(512, 384), b16(2, 512, 384),
            dma((5,)), dma((3,)), dma((len(PIECES),)), dma((ARRIVALS,)), dma((1,)), dma((4,)),
            dma((1,)), dma((3, 2)), dma((1,)), dma((4,)), dma((1,)), dma((1,)),
            dma((2,)), dma((2, 4)),
            dma((1,)), dma((1,)), dma((1,)), dma((1,)), dma((1,)), dma((1,)),
            dma, dma((4, 2)), dma((1,)), dma((3, 2)),
        ],
        compiler_params=pltpu.CompilerParams(
            collective_id=0, has_side_effects=True, vmem_limit_bytes=VMEM_BYTES
        ),
        name="project_attend_mix",
    )(
        row_counts, row_places, head_gain.reshape(1, -1), enc_rows, stream,
        norm_gain.reshape(1, -1), proj_in, proj_out.T, mix_weight.T, qkv_weight.transpose(1, 0, 2),
    )


def solution(mesh):
    in_specs = (
        P(("ctx", "head"), None),
        P("ctx", None),
        P("ctx", None),
        P("ctx", None),
        P(),
        P("ctx", "head"),
        P("head", "ctx"),
        P(None, None, "head"),
        P("head"),
        P("head", "ctx"),
    )
    out_specs = P("ctx", "head")
    return jax.shard_map(
        on_device, mesh=mesh, in_specs=in_specs, out_specs=out_specs, check_vma=False
    )
```
